256 devices in a mesh: dp: 64 (over y, z, x_lo), space: 4 (over x_hi, core).
Axes of the slice: x: 4 (x_hi: 2, x_lo: 2; x = x_hi * 2 + x_lo), y: 4, z: 8, core: 2. Of those that a mesh axis runs over, the one named last changes fastest.
Arguments:
- volumes: bfloat16 [256, 32, 64, 512], P('dp', None, 'space'), may hold values from -6 to 6
- first_kernel: bfloat16 [27, 32, 64], replicated, may hold values from -0.21875 to 0.21875
- second_kernel: bfloat16 [27, 64, 128], replicated, may hold values from -0.15625 to 0.15625
- upstream: bfloat16 [256, 128, 16, 32], P(('dp', 'space')), may hold values from -6 to 6
Outputs:
- features: bfloat16 [256, 128, 16, 32], P(('dp', 'space'))
- first_grad: float32 [27, 32, 64], replicated
- second_grad: float32 [27, 64, 128], replicated
The draws below stay inside these ranges and needn't reach their ends.
All inputs are finite; a program needn't handle non-finite values.
Results may differ from the reference program's by a relative error of at most 0.0059.
Values may be sent and summed in bfloat16 or wider, within the bound.
No kernel may reach another device: no remote copies, remote signals or barrier semaphores. Data moves between devices by JAX's collectives and lax.ppermute only.
A program may use at most 64 MiB of HBM per device.

```python
import jax
import jax.numpy as jnp
from jax import lax

C0 = 32
C1 = 64
C2 = 128
XD = 64
YD = 32
ZD = 16
SAMPLES = 256


def steps_of(rng, shape, split, smallest, high):
    gain = 1.0
    for axis_at, blocks in split:
        steps = jax.random.uniform(jax.random.fold_in(jax.random.fold_in(rng, 6), axis_at), (blocks,), jnp.float32, smallest / len(split), high / len(split))
        gain = gain * jnp.repeat(jnp.exp(steps), shape[axis_at] // blocks).reshape((-1,) + (1,) * (len(shape) - 1 - axis_at))
    return gain


def normal_values(rng, shape, spread, reach, cuts=(), kind=jnp.bfloat16):
    gain = steps_of(rng, shape, cuts, -0.22, 0.18) if cuts else 1.0
    drawn = jax.random.normal(rng, shape, jnp.float32) * spread * gain
    return jnp.minimum(jnp.maximum(drawn, -reach), reach).astype(kind)


def setup_inputs(seed: int = 0) -> dict:
    arg_keys = jax.random.split(jax.random.key(seed), 5)
    return {
        "volumes": normal_values(arg_keys[0], (SAMPLES, C0, XD, YD * ZD), 1.0, 6.0, ((0, 64), (2, 4))),
        "first_kernel": normal_values(arg_keys[1], (27, C0, C1), (27 * C0) ** -0.5, 0.21875),
        "second_kernel": normal_values(arg_keys[2], (27, C1, C2), (27 * C1) ** -0.5, 0.15625),
        "upstream": normal_values(arg_keys[3], (SAMPLES, C2, XD // 4, YD * ZD // 16), 1.0, 6.0, ((0, 256),)),
    }


def smooth_act(value):
    return 0.3 * value + 0.7 * jax.nn.softplus(value)

def smooth_slope(value):
    return 0.3 + 0.7 * jax.nn.sigmoid(value)

def pad_low(value):
    return jnp.pad(value, ((0, 0), (0, 0), (1, 0), (1, 0), (1, 0)))

def tap_view(padded, first, second, third, shape_out):
    ox, oy, oz = shape_out
    return padded[:, :, first:first + 2 * ox:2, second:second + 2 * oy:2, third:third + 2 * oz:2]

def forward_conv(padded, kernel, shape_out):
    total = None
    for first in range(3):
        for second in range(3):
            for third in range(3):
                piece = tap_view(padded, first, second, third, shape_out).astype(jnp.float32)
                term = jnp.einsum('scxyz,co->soxyz', piece, kernel[first * 9 + second * 3 + third].astype(jnp.float32))
                total = term if total is None else total + term
    return total

def kernel_grad(padded, delta):
    shape_out = delta.shape[2:]
    rows = []
    for first in range(3):
        for second in range(3):
            for third in range(3):
                piece = tap_view(padded, first, second, third, shape_out).astype(jnp.float32)
                rows.append(jnp.einsum('scxyz,soxyz->co', piece, delta.astype(jnp.float32)))
    return jnp.stack(rows, 0)

def input_grad(delta, kernel, padded_shape):
    ox, oy, oz = delta.shape[2:]
    total = jnp.zeros((padded_shape[0], kernel.shape[1]) + tuple(padded_shape[2:]), jnp.float32)
    for first in range(3):
        for second in range(3):
            for third in range(3):
                term = jnp.einsum('soxyz,co->scxyz', delta.astype(jnp.float32), kernel[first * 9 + second * 3 + third].astype(jnp.float32))
                total = total.at[:, :, first:first + 2 * ox:2, second:second + 2 * oy:2, third:third + 2 * oz:2].add(term)
    return total

def reference(volumes, first_kernel, second_kernel, upstream):
    scale = 1.0 / SAMPLES

    def one_sample(carry, items):
        grad_one, grad_two = carry
        sample, cot = items
        padded = pad_low(sample.reshape(1, C0, XD, YD, ZD))
        pre_first = forward_conv(padded, first_kernel, (XD // 2, YD // 2, ZD // 2))
        hidden = smooth_act(pre_first).astype(jnp.bfloat16)
        hidden_pad = pad_low(hidden)
        pre_second = forward_conv(hidden_pad, second_kernel, (XD // 4, YD // 4, ZD // 4))
        features = smooth_act(pre_second).astype(jnp.bfloat16)
        delta_second = (cot.reshape(1, C2, XD // 4, YD // 4, ZD // 4).astype(jnp.float32) * smooth_slope(pre_second)).astype(jnp.bfloat16)
        grad_two = grad_two + scale * kernel_grad(hidden_pad, delta_second)
        back = input_grad(delta_second, second_kernel, hidden_pad.shape)
        back_hidden = back[:, :, 1:, 1:, 1:].astype(jnp.bfloat16)
        delta_first = (back_hidden.astype(jnp.float32) * smooth_slope(pre_first)).astype(jnp.bfloat16)
        grad_one = grad_one + scale * kernel_grad(padded, delta_first)
        return ((grad_one, grad_two), features.reshape(C2, XD // 4, YD * ZD // 16))
    start = (jnp.zeros((27, C0, C1), jnp.float32), jnp.zeros((27, C1, C2), jnp.float32))
    (first_grad, second_grad), features = lax.scan(one_sample, start, (volumes, upstream))
    return (features, first_grad, second_grad)
```

```python
import jax
import jax.numpy as jnp
from jax import lax
from jax.sharding import Mesh
from jax.sharding import PartitionSpec as P

YD = 32
ZD = 16
DP = ("y", "z", "xl")
SPACE = ("xh", "c")


def shifted(value, axis, steps):
    count = lax.axis_size(axis)
    initial, last = (max(0, -steps), min(count, count - steps))
    return lax.ppermute(value, axis, [(source, source + steps) for source in range(initial, last)])


def smooth_act(value):
    return 0.3 * value + 0.7 * jax.nn.softplus(value)


def smooth_slope(value):
    return 0.3 + 0.7 * jax.nn.sigmoid(value)


def plane_table(size_y, size_z):
    half_y = size_y // 2
    half_z = size_z // 2
    cells = jnp.arange(half_y * half_z, dtype=jnp.int32)
    out_y = cells // half_z
    out_z = cells % half_z
    source = jnp.arange(size_y * size_z, dtype=jnp.int32)[:, None]
    blocks = []
    for second in range(3):
        for third in range(3):
            read_y = 2 * out_y + second - 1
            read_z = 2 * out_z + third - 1
            index = jnp.where((read_y >= 0) & (read_z >= 0), read_y * size_z + read_z, -1)
            blocks.append((source == index[None, :]).astype(jnp.bfloat16))
    return jnp.concatenate(blocks, 1)


def tap_planes(padded, table):
    return jnp.dot(padded, table, preferred_element_type=jnp.bfloat16)


def tap_rows(planes, first, out_rows):
    group, chans, rows, width = planes.shape
    picked = planes[:, :, first : first + 2 * out_rows : 2]
    return picked.reshape(group, chans, out_rows, 9, width // 9)


def forward_conv(planes, kernel, out_rows):
    total = None
    for first in range(3):
        rows = tap_rows(planes, first, out_rows)
        term = jnp.einsum(
            "scxtm,tco->soxm",
            rows,
            kernel[9 * first : 9 * first + 9],
            preferred_element_type=jnp.float32,
        )
        total = term if total is None else total + term
    return total


def kernel_grad(planes, delta):
    out_rows = delta.shape[2]
    blocks = []
    for first in range(3):
        rows = tap_rows(planes, first, out_rows)
        blocks.append(
            jnp.einsum("scxtm,soxm->tco", rows, delta, preferred_element_type=jnp.float32)
        )
    return jnp.concatenate(blocks, 0)


def input_grad(delta, kernel, table):
    group, outs, out_rows, cells = delta.shape
    chans = kernel.shape[1]
    width = 9 * cells
    parts = []
    for first in range(3):
        term = jnp.einsum(
            "soxm,tco->scxtm",
            delta,
            kernel[9 * first : 9 * first + 9],
            preferred_element_type=jnp.float32,
        )
        parts.append(term.reshape(group, chans, out_rows, width))
    zero_row = jnp.zeros((group, chans, 1, width), jnp.float32)
    even = jnp.concatenate([parts[0], zero_row], 2) + jnp.concatenate([zero_row, parts[2]], 2)
    woven = jnp.stack([even[:, :, :out_rows], parts[1]], 3).reshape(
        group, chans, 2 * out_rows, width
    )
    grad_planes = jnp.concatenate([woven, even[:, :, out_rows:]], 2)
    return jnp.dot(grad_planes, table.T.astype(jnp.float32), precision=lax.Precision.HIGHEST)


X_GROUP = ("xl", "xh", "c")
LANES = 128
ROWS = 2304


def exchange(chunks, axis):
    return lax.all_to_all(chunks, axis, split_axis=0, concat_axis=0, tiled=True)


def reduce_stage(rows, axis, parts):
    got = exchange(rows.reshape(parts, -1, LANES), axis)
    return jnp.sum(got.astype(jnp.float32), 0).astype(jnp.bfloat16)


def gather_stage(rows, axis, parts):
    copies = jnp.broadcast_to(rows[None], (parts,) + rows.shape)
    return exchange(copies, axis).reshape(-1, LANES)


def sum_everywhere(first_term, second_term):
    taps, ins, outs = first_term.shape
    flat = first_term.reshape(taps * ins, outs)
    half = flat.shape[0] // 2
    packed = jnp.concatenate([flat[:half], flat[half:]], 1)
    wide = second_term.reshape(-1, LANES)
    used = half + wide.shape[0]
    pad = jnp.zeros((ROWS - used, LANES), jnp.float32)
    rows = jnp.concatenate([wide, packed, pad], 0).astype(jnp.bfloat16)
    rows = reduce_stage(rows, X_GROUP, 8)
    rows = reduce_stage(rows, "y", 4)
    got = exchange(jnp.broadcast_to(rows[None], (8,) + rows.shape), "z")
    rows = jnp.sum(got.astype(jnp.float32), 0).astype(jnp.bfloat16)
    rows = gather_stage(rows, "y", 4)
    rows = gather_stage(rows, X_GROUP, 8).astype(jnp.float32)
    second = rows[: wide.shape[0]].reshape(second_term.shape)
    packed = rows[wide.shape[0] : used]
    flat = jnp.concatenate([packed[:, :outs], packed[:, outs:]], 0)
    return flat.reshape(first_term.shape), second


def per_device(volumes, first_kernel, second_kernel, upstream):
    group = volumes.shape[0]
    rows_in = volumes.shape[2]
    mid_ch = first_kernel.shape[2]
    scale = 1.0 / (group * lax.axis_size(DP))
    first_table = plane_table(YD, ZD)
    second_table = plane_table(YD // 2, ZD // 2)
    rim = shifted(volumes[:, :, -1:, :], SPACE, 1)
    padded = jnp.concatenate([rim, volumes], 2)
    first_planes = tap_planes(padded, first_table)
    pre_first = forward_conv(first_planes, first_kernel, rows_in // 2)
    hidden = smooth_act(pre_first).astype(jnp.bfloat16)
    whole = lax.all_to_all(hidden, SPACE, split_axis=0, concat_axis=2, tiled=True)
    full_rows = whole.shape[2]
    zero_layer = jnp.zeros((whole.shape[0], mid_ch, 1, whole.shape[3]), jnp.bfloat16)
    hidden_pad = jnp.concatenate([zero_layer, whole], 2)
    second_planes = tap_planes(hidden_pad, second_table)
    pre_second = forward_conv(second_planes, second_kernel, full_rows // 2)
    features = smooth_act(pre_second).astype(jnp.bfloat16)
    delta_second = (upstream.astype(jnp.float32) * smooth_slope(pre_second)).astype(jnp.bfloat16)
    second_term = scale * kernel_grad(second_planes, delta_second)
    back = input_grad(delta_second, second_kernel, second_table)
    back_whole = back[:, :, 1:].astype(jnp.bfloat16)
    back_hidden = lax.all_to_all(back_whole, SPACE, split_axis=2, concat_axis=0, tiled=True)
    delta_first = (back_hidden.astype(jnp.float32) * smooth_slope(pre_first)).astype(jnp.bfloat16)
    first_term = scale * kernel_grad(first_planes, delta_first)
    first_grad, second_grad = sum_everywhere(first_term, second_term)
    return (features, first_grad, second_grad)


def solution(mesh):
    fine = Mesh(mesh.devices.reshape(4, 8, 2, 2, 2), ("y", "z", "xl", "xh", "c"))
    in_specs = (P(DP, None, SPACE, None), P(), P(), P(DP + SPACE, None, None, None))
    out_specs = (P(DP + SPACE, None, None, None), P(), P())
    return jax.shard_map(
        per_device, mesh=fine, in_specs=in_specs, out_specs=out_specs, check_vma=False
    )
```

```python
import jax
import jax.numpy as jnp
import numpy as np
from jax import lax
from jax.experimental import pallas as pl
from jax.experimental.pallas import tpu as pltpu
from jax.sharding import Mesh
from jax.sharding import PartitionSpec as P

YD = 32
ZD = 16
LANES = 128
DP = ("y", "z", "xl")
SPACE = ("xh", "c")
X_GROUP = ("xl", "xh", "c")
BF = jnp.bfloat16
F32 = jnp.float32
INTERPRET = False


def shifted(value, axis, steps):
    count = lax.axis_size(axis)
    initial, last = (max(0, -steps), min(count, count - steps))
    return lax.ppermute(value, axis, [(source, source + steps) for source in range(initial, last)])


def plane_table(size_y, size_z, copies):
    half_y, half_z = size_y // 2, size_z // 2
    cells = half_y * half_z
    table = np.zeros((copies, size_y * size_z, 9, copies, cells), np.float32)
    for second in range(3):
        for third in range(3):
            for out_y in range(half_y):
                for out_z in range(half_z):
                    y, z = 2 * out_y + second - 1, 2 * out_z + third - 1
                    if y >= 0 and z >= 0:
                        for k in range(copies):
                            table[k, y * size_z + z, 3 * second + third, k, out_y * half_z + out_z] = 1
    return jnp.asarray(table.reshape(copies * size_y * size_z, 9 * copies * cells), BF)


def row_order(chans, rows):
    shape = (rows * chans, chans * rows)
    at = lax.broadcasted_iota(jnp.int32, shape, 0)
    source = lax.broadcasted_iota(jnp.int32, shape, 1)
    block = at // chans
    row = (block % (rows // 2)) * 2 + block // (rows // 2)
    return (source == (at % chans) * rows + row).astype(F32).astype(BF)


def turned(value):
    size = value.shape[1]
    row = lax.broadcasted_iota(jnp.int32, (size, size), 0)
    col = lax.broadcasted_iota(jnp.int32, (size, size), 1)
    return dot_nt((row == col).astype(F32).astype(BF), value)


def dot(a, b):
    return jnp.dot(a, b, preferred_element_type=F32)


def dot_nt(a, b):
    return lax.dot_general(a, b, (((1,), (1,)), ((), ())), preferred_element_type=F32)


def act_and_slope(v):
    e = jnp.exp(-jnp.abs(v))
    act = 0.3 * v + 0.7 * (jnp.maximum(v, 0.0) + jnp.log(1.0 + e))
    slope = 0.3 + 0.7 * jnp.where(v >= 0, 1.0, e) / (1.0 + e)
    return act, slope


def first_body(v_ref, table_ref, w_ref, im_ref, pre_ref, order_ref, wt_ref, z_ref):
    @pl.when(pl.program_id(0) == 0)
    def _():
        order_ref[...] = row_order(32, 16)
        wt_ref[...] = turned(w_ref[...]).astype(BF)

    v = v_ref[0].reshape(512, 512)
    rows = dot(order_ref[...], v).astype(BF)
    z_ref[...] = dot(rows, table_ref[...]).astype(BF)
    for o1 in range(8):
        for a in range(3):
            x = 2 * o1 + a - 1
            for t in range(9):
                if x < 0:
                    block = jnp.zeros((32, LANES), BF)
                else:
                    at = ((x % 2) * 8 + x // 2) * 32
                    block = z_ref[at : at + 32, t * LANES : (t + 1) * LANES]
                k = (9 * a + t) * 32
                im_ref[0, k : k + 32, o1 * LANES : (o1 + 1) * LANES] = block
    pre_ref[0] = dot(wt_ref[...], im_ref[0])


def rim_body(pre_ref, rim_ref, table_ref, w_ref, hid_ref, last_ref, slope_ref, rimz_ref):
    z = dot(rim_ref[...].reshape(128, 512), table_ref[...]).astype(BF)
    wt = turned(w_ref[:288]).astype(BF)
    for s in range(4):
        im = jnp.concatenate(
            [z[32 * s : 32 * s + 32, t * LANES : (t + 1) * LANES] for t in range(9)], 0
        )
        rimz_ref[s] = im
        extra = dot(wt, im)
        for r in range(8):
            lanes = slice(r * LANES, (r + 1) * LANES)
            pre = pre_ref[s, :, lanes]
            if r == 0:
                pre = pre + extra
            act, slope = act_and_slope(pre)
            hidden = act.astype(BF)
            hid_ref[s, :, lanes] = hidden
            slope_ref[s, :, lanes] = slope
            if r == 7:
                last_ref[s] = hidden


def second_body(hid_ref, table_ref, w_ref, im_ref, pre_ref):
    for s in range(4):
        row = lambda r: (
            hid_ref[s, :, r * LANES : (r + 1) * LANES] if r >= 0 else jnp.zeros((64, LANES), BF)
        )
        left = jnp.concatenate(
            [jnp.concatenate([row(2 * o1 + a - 1) for o1 in range(4)], 1) for a in range(3)], 0
        )
        z = dot(left, table_ref[...]).astype(BF)
        for a in range(3):
            for t in range(9):
                k = (9 * a + t) * 64
                im_ref[k : k + 64, s * LANES : (s + 1) * LANES] = z[
                    64 * a : 64 * a + 64, t * LANES : (t + 1) * LANES
                ]
    pre_ref[...] = dot(turned(w_ref[...]).astype(BF), im_ref[...])


def halo_body(halo_ref, pre_ref, up_ref, table_ref, w_ref, feat_ref, delta_ref, edge_ref, imh_ref):
    z = dot(halo_ref[...].reshape(256, LANES), table_ref[:LANES, :]).astype(BF)
    for s in range(4):
        for t in range(9):
            imh_ref[t * 64 : t * 64 + 64, s * LANES : (s + 1) * LANES] = z[
                64 * s : 64 * s + 64, t * LANES : (t + 1) * LANES
            ]
    pre = pre_ref[...] + dot(turned(w_ref[:576]).astype(BF), imh_ref[...])
    lane = lax.broadcasted_iota(jnp.int32, (128, LANES), 1)
    edge = jnp.zeros((128, LANES), F32)
    for s in range(4):
        act, slope = act_and_slope(pre[:, s * LANES : (s + 1) * LANES])
        feat_ref[s] = turned(act.astype(BF)).astype(BF)
        delta = (turned(up_ref[s]) * slope).astype(BF)
        delta_ref[:, s * LANES : (s + 1) * LANES] = delta
        moved = delta.astype(F32)
        if s:
            moved = pltpu.roll(moved, 32 * s, 1)
        edge = jnp.where(lane // 32 == s, moved, edge)
    edge_ref[...] = edge.astype(BF)


def second_grad_body(im_ref, imh_ref, delta_ref, out_ref):
    scale = 1.0 / 256
    delta = delta_ref[...]
    out_ref[:576] = (dot_nt(im_ref[:576] + imh_ref[...], delta) * scale).astype(BF)
    out_ref[576:] = (dot_nt(im_ref[576:], delta) * scale).astype(BF)


def back_body(
    delta_ref, edge_ref, k_ref, table_ref, slope_ref, im_ref, rimz_ref, out_ref, kodd_ref, acc_ref
):
    s = pl.program_id(0)

    @pl.when(s == 0)
    def _():
        acc_ref[...] = jnp.zeros_like(acc_ref)
        kodd_ref[:, :128] = k_ref[:576]
        kodd_ref[:, 128:] = k_ref[1152:]

    lane = lax.broadcasted_iota(jnp.int32, (128, LANES), 1)
    own = delta_ref[...]
    moved = pltpu.roll(own.astype(F32), 96, 1)
    rim = edge_ref[...].astype(F32)
    ends = rim
    for k in range(3):
        ends = jnp.where(s == k, pltpu.roll(rim, 96 - 32 * k, 1), ends)
    ahead = jnp.where(lane < 96, moved, ends).astype(BF)
    even = dot(k_ref[576:1152], own)
    odd = dot(kodd_ref[...], jnp.concatenate([ahead, own], 0))
    parts = []
    for grad in (even, odd):
        flat = jnp.concatenate([grad[64 * t : 64 * t + 64] for t in range(9)], 1)
        high = flat.astype(BF)
        parts += [high, (flat - high.astype(F32)).astype(BF)]
    got = dot_nt(jnp.concatenate(parts, 0), table_ref[...])
    rows = []
    for r in range(8):
        base = 128 * (r % 2)
        lanes = slice((r // 2) * LANES, (r // 2 + 1) * LANES)
        back = (got[base : base + 64, lanes] + got[base + 64 : base + 128, lanes]).astype(BF)
        slope = slope_ref[0, :, r * LANES : (r + 1) * LANES]
        rows.append((back.astype(F32) * slope).astype(BF))
    delta_first = jnp.concatenate(rows, 1)
    term = dot_nt(im_ref[0], delta_first)
    rim_term = dot_nt(rimz_ref[0], rows[0])

    acc_ref[...] += term
    acc_ref[:288] += rim_term

    @pl.when(s == 3)
    def _():
        acc = acc_ref[...] * (1.0 / 256)
        out_ref[...] = jnp.concatenate([acc[:432], acc[432:]], 1).astype(BF)


def finish_body(rows_ref, first_ref, second_ref):
    second_ref[...] = rows_ref[:1728].astype(F32)
    packed = rows_ref[1728:2160].astype(F32)
    first_ref[:432] = packed[:, :64]
    first_ref[432:] = packed[:, 64:]


def call(body, outs, ins=None, grid=(), out_specs=None, scratch=(), mib=16):
    whole = lambda shape: pl.BlockSpec(shape, lambda *_: (0,) * len(shape))

    def run(*args):
        in_specs = [
            whole(arg.shape) if spec is None else spec
            for arg, spec in zip(args, ins or (None,) * len(args))
        ]
        shapes = [
            pltpu.HBM(*out[:2]) if out[2:] and not INTERPRET else jax.ShapeDtypeStruct(*out[:2])
            for out in outs
        ]
        return pl.pallas_call(
            body,
            grid=grid,
            in_specs=in_specs,
            out_specs=out_specs or [whole(out[0]) for out in outs],
            out_shape=shapes,
            scratch_shapes=list(scratch),
            compiler_params=pltpu.CompilerParams(vmem_limit_bytes=mib * 1024 * 1024),
            interpret=INTERPRET,
        )(*args)

    return run


def exchange(chunks, axis):
    return lax.all_to_all(chunks, axis, split_axis=0, concat_axis=0, tiled=True)


def reduce_stage(rows, axis):
    got = exchange(rows.reshape(lax.axis_size(axis), -1, LANES), axis)
    return jnp.sum(got.astype(F32), 0).astype(BF)


def gather_stage(rows, axis):
    copies = jnp.broadcast_to(rows[None], (lax.axis_size(axis),) + rows.shape)
    return exchange(copies, axis).reshape(-1, LANES)


def sum_everywhere(packed, wide, features):
    pad = jnp.zeros((144, LANES), BF)
    rows = jnp.concatenate([wide, packed, pad], 0).reshape(lax.axis_size(X_GROUP), -1, LANES)
    chunk = rows.shape[1]
    twin = lax.axis_size("xl")
    feats = jnp.concatenate([features] * twin, 0)
    got = exchange(jnp.concatenate([rows, feats], 1), X_GROUP)
    mine = lax.dynamic_slice_in_dim(got, 4 * lax.axis_index("xl"), 4, 0)[:, chunk:]
    rows = jnp.sum(got[:, :chunk].astype(F32), 0).astype(BF)
    rows = reduce_stage(rows, "y")
    got = exchange(jnp.broadcast_to(rows[None], (lax.axis_size("z"),) + rows.shape), "z")
    rows = jnp.sum(got.astype(F32), 0).astype(BF)
    rows = gather_stage(rows, "y")
    rows = gather_stage(rows, X_GROUP)
    first, second = call(finish_body, [((864, 64), F32), ((1728, 128), F32)])(rows)
    return first.reshape(27, 32, 64), second.reshape(27, 64, 128), mine


def per_device(volumes, first_kernel, second_kernel, upstream):
    table = plane_table(YD, ZD, 1)
    table2 = plane_table(YD // 2, ZD // 2, 4)
    rim = shifted(volumes[:, :, 15, :], SPACE, 1)
    up = exchange(upstream.reshape(128, 4, 128).transpose(1, 2, 0), SPACE)
    w1 = first_kernel.reshape(864, 64)
    k2 = second_kernel.reshape(1728, 128)
    volumes = pltpu.with_memory_space_constraint(volumes, pltpu.HBM)
    im1, pre1 = call(
        first_body,
        [((4, 864, 1024), BF, True), ((4, 64, 1024), F32)],
        ins=(pl.BlockSpec((1, 32, 16, 512), lambda s: (s, 0, 0, 0)), None, None),
        grid=(4,),
        out_specs=[
            pl.BlockSpec((1, 864, 1024), lambda s: (s, 0, 0)),
            pl.BlockSpec((1, 64, 1024), lambda s: (s, 0, 0)),
        ],
        scratch=[
            pltpu.VMEM((512, 512), BF),
            pltpu.VMEM((64, 864), BF),
            pltpu.VMEM((512, 1152), BF),
        ],
    )(volumes, table, w1)
    hidden, last, slope1, rimz = call(
        rim_body,
        [
            ((4, 64, 1024), BF),
            ((4, 64, 128), BF),
            ((4, 64, 1024), F32, True),
            ((4, 288, 128), BF),
        ],
    )(pre1, rim, table, w1)
    halo = shifted(last, SPACE, 1)
    im2, pre2 = call(second_body, [((1728, 512), BF, True), ((128, 512), F32)])(hidden, table2, k2)
    features, delta2, edge, im2h = call(
        halo_body,
        [((4, 128, 128), BF), ((128, 512), BF), ((128, 128), BF), ((576, 512), BF)],
    )(halo, pre2, up, table2, k2)
    edge = shifted(edge, SPACE, -1)
    (wide,) = call(second_grad_body, [((1728, 128), BF)])(im2, im2h, delta2)
    (packed,) = call(
        back_body,
        [((432, 128), BF)],
        ins=(
            pl.BlockSpec((128, 128), lambda s: (0, s)),
            None,
            None,
            None,
            pl.BlockSpec((1, 64, 1024), lambda s: (s, 0, 0)),
            pl.BlockSpec((1, 864, 1024), lambda s: (s, 0, 0)),
            pl.BlockSpec((1, 288, 128), lambda s: (s, 0, 0)),
        ),
        grid=(4,),
        scratch=[pltpu.VMEM((576, 256), BF), pltpu.VMEM((864, 64), F32)],
    )(delta2, edge, k2, table2, slope1, im1, rimz)
    first_grad, second_grad, features = sum_everywhere(packed, wide, features)
    features = features.transpose(2, 0, 1).reshape(1, 128, 16, 32)
    return (features, first_grad, second_grad)


def solution(mesh):
    fine = Mesh(mesh.devices.reshape(4, 8, 2, 2, 2), ("y", "z", "xl", "xh", "c"))
    in_specs = (P(DP, None, SPACE, None), P(), P(), P(DP + SPACE, None, None, None))
    out_specs = (P(DP + SPACE, None, None, None), P(), P())
    return jax.shard_map(
        per_device, mesh=fine, in_specs=in_specs, out_specs=out_specs, check_vma=False
    )
```

```python
import jax
import jax.numpy as jnp
import numpy as np
from jax import lax
from jax.experimental import pallas as pl
from jax.experimental.pallas import tpu as pltpu
from jax.sharding import Mesh
from jax.sharding import PartitionSpec as P

YD = 32
ZD = 16
LANES = 128
DP = ("y", "z", "xl")
SPACE = ("xh", "c")
XY_GROUP = ("y", "xl", "xh", "c")
BF = jnp.bfloat16
F32 = jnp.float32
INTERPRET = False


def shifted(value, axis, steps):
    count = lax.axis_size(axis)
    initial, last = (max(0, -steps), min(count, count - steps))
    return lax.ppermute(value, axis, [(source, source + steps) for source in range(initial, last)])


def plane_table(size_y, size_z, copies):
    half_y, half_z = size_y // 2, size_z // 2
    cells = half_y * half_z
    table = np.zeros((copies, size_y * size_z, 9, copies, cells), np.float32)
    for second in range(3):
        for third in range(3):
            for out_y in range(half_y):
                for out_z in range(half_z):
                    y, z = 2 * out_y + second - 1, 2 * out_z + third - 1
                    if y >= 0 and z >= 0:
                        for k in range(copies):
                            table[k, y * size_z + z, 3 * second + third, k, out_y * half_z + out_z] = 1
    return jnp.asarray(table.reshape(copies * size_y * size_z, 9 * copies * cells), BF)


def row_order(chans, rows):
    shape = (rows * chans, chans * rows)
    at = lax.broadcasted_iota(jnp.int32, shape, 0)
    source = lax.broadcasted_iota(jnp.int32, shape, 1)
    block = at // chans
    row = (block % (rows // 2)) * 2 + block // (rows // 2)
    return (source == (at % chans) * rows + row).astype(F32).astype(BF)


def turned(value):
    size = value.shape[1]
    row = lax.broadcasted_iota(jnp.int32, (size, size), 0)
    col = lax.broadcasted_iota(jnp.int32, (size, size), 1)
    return dot_nt((row == col).astype(F32).astype(BF), value)


def dot(a, b):
    return jnp.dot(a, b, preferred_element_type=F32)


def dot_nt(a, b):
    return lax.dot_general(a, b, (((1,), (1,)), ((), ())), preferred_element_type=F32)


def act_and_slope(v):
    e = jnp.exp(-jnp.abs(v))
    act = 0.3 * v + 0.7 * (jnp.maximum(v, 0.0) + jnp.log(1.0 + e))
    slope = 0.3 + 0.7 * jnp.where(v >= 0, 1.0, e) / (1.0 + e)
    return act, slope


def first_body(v_ref, table_ref, w_ref, im_ref, pre_ref, order_ref, z_ref):
    order_ref[...] = row_order(32, 16)
    wt = turned(w_ref[...]).astype(BF)

    def one(s, carry):
        rows = dot(order_ref[...], v_ref[s].reshape(512, 512)).astype(BF)
        z_ref[...] = dot(rows, table_ref[...]).astype(BF)
        for o1 in range(8):
            for a in range(3):
                x = 2 * o1 + a - 1
                for t in range(9):
                    if x < 0:
                        block = jnp.zeros((32, LANES), BF)
                    else:
                        at = ((x % 2) * 8 + x // 2) * 32
                        block = z_ref[at : at + 32, t * LANES : (t + 1) * LANES]
                    k = (9 * a + t) * 32
                    im_ref[s, k : k + 32, o1 * LANES : (o1 + 1) * LANES] = block
        pre_ref[s] = dot(wt, im_ref[s])
        return carry

    lax.fori_loop(0, 4, one, 0)


def rim_body(pre_ref, rim_ref, table_ref, w_ref, hid_ref, last_ref, slope_ref, rimz_ref):
    z = dot(rim_ref[...].reshape(128, 512), table_ref[...]).astype(BF)
    wt = turned(w_ref[:288]).astype(BF)
    for s in range(4):
        im = jnp.concatenate(
            [z[32 * s : 32 * s + 32, t * LANES : (t + 1) * LANES] for t in range(9)], 0
        )
        rimz_ref[s] = im
        extra = dot(wt, im)
        for r in range(8):
            lanes = slice(r * LANES, (r + 1) * LANES)
            pre = pre_ref[s, :, lanes]
            if r == 0:
                pre = pre + extra
            act, slope = act_and_slope(pre)
            hidden = act.astype(BF)
            hid_ref[s, :, lanes] = hidden
            slope_ref[s, :, lanes] = slope
            if r == 7:
                last_ref[s] = hidden


def second_body(hid_ref, table_ref, w_ref, im_ref, pre_ref):
    for s in range(4):
        row = lambda r: (
            hid_ref[s, :, r * LANES : (r + 1) * LANES] if r >= 0 else jnp.zeros((64, LANES), BF)
        )
        left = jnp.concatenate(
            [jnp.concatenate([row(2 * o1 + a - 1) for o1 in range(4)], 1) for a in range(3)], 0
        )
        z = dot(left, table_ref[...]).astype(BF)
        for a in range(3):
            for t in range(9):
                k = (9 * a + t) * 64
                im_ref[k : k + 64, s * LANES : (s + 1) * LANES] = z[
                    64 * a : 64 * a + 64, t * LANES : (t + 1) * LANES
                ]
    pre_ref[...] = dot(turned(w_ref[...]).astype(BF), im_ref[...])


def pick_body(me_ref, up_ref, *out_refs):
    for m in range(4):
        out_refs[m][...] = up_ref[me_ref[0] ^ m]


def halo_body(me_ref, halo_ref, pre_ref, up0, up1, up2, up3, table_ref, w_ref, *refs):
    feat_refs, (delta_ref, edge_ref, imh_ref, up_ref, feat_ref) = refs[:4], refs[4:]
    me = me_ref[0]
    for m, ref in enumerate((up0, up1, up2, up3)):
        up_ref[me ^ m] = ref[...]
    z = dot(halo_ref[...].reshape(256, LANES), table_ref[:LANES, :]).astype(BF)
    for s in range(4):
        for t in range(9):
            imh_ref[t * 64 : t * 64 + 64, s * LANES : (s + 1) * LANES] = z[
                64 * s : 64 * s + 64, t * LANES : (t + 1) * LANES
            ]
    pre = pre_ref[...] + dot(turned(w_ref[:576]).astype(BF), imh_ref[...])
    lane = lax.broadcasted_iota(jnp.int32, (128, LANES), 1)
    edge = jnp.zeros((128, LANES), F32)
    for s in range(4):
        act, slope = act_and_slope(pre[:, s * LANES : (s + 1) * LANES])
        feat_ref[s] = turned(act.astype(BF)).astype(BF)
        delta = (turned(up_ref[s]) * slope).astype(BF)
        delta_ref[s] = delta
        moved = delta.astype(F32)
        if s:
            moved = pltpu.roll(moved, 32 * s, 1)
        edge = jnp.where(lane // 32 == s, moved, edge)
    edge_ref[...] = edge.astype(BF)
    for m in range(4):
        feat_refs[m][...] = feat_ref[me ^ m]


def second_grad_body(im_ref, imh_ref, delta_ref, out_ref):
    scale = 1.0 / 256
    delta = jnp.concatenate([delta_ref[s] for s in range(4)], 1)
    out_ref[:576] = (dot_nt(im_ref[:576] + imh_ref[...], delta) * scale).astype(BF)
    out_ref[576:] = (dot_nt(im_ref[576:], delta) * scale).astype(BF)


def back_body(
    delta_ref, edge_ref, k_ref, table_ref, slope_ref, im_ref, rimz_ref, out_ref, kodd_ref, ahead_ref, acc_ref
):
    lane = lax.broadcasted_iota(jnp.int32, (128, LANES), 1)
    acc_ref[...] = jnp.zeros_like(acc_ref)
    kodd_ref[:, :128] = k_ref[:576]
    kodd_ref[:, 128:] = k_ref[1152:]
    rim = edge_ref[...].astype(F32)
    for s in range(4):
        own = delta_ref[s]
        moved = pltpu.roll(own.astype(F32), 96, 1)
        ends = pltpu.roll(rim, 96 - 32 * s, 1) if s != 3 else rim
        ahead_ref[s, :128] = jnp.where(lane < 96, moved, ends).astype(BF)
        ahead_ref[s, 128:] = own

    def one(s, carry):
        even = dot(k_ref[576:1152], delta_ref[s])
        odd = dot(kodd_ref[...], ahead_ref[s])
        parts = []
        for grad in (even, odd):
            flat = jnp.concatenate([grad[64 * t : 64 * t + 64] for t in range(9)], 1)
            high = flat.astype(BF)
            parts += [high, (flat - high.astype(F32)).astype(BF)]
        got = dot_nt(jnp.concatenate(parts, 0), table_ref[...])
        rows = []
        for r in range(8):
            base = 128 * (r % 2)
            lanes = slice((r // 2) * LANES, (r // 2 + 1) * LANES)
            back = (got[base : base + 64, lanes] + got[base + 64 : base + 128, lanes]).astype(BF)
            slope = slope_ref[s, :, r * LANES : (r + 1) * LANES]
            rows.append((back.astype(F32) * slope).astype(BF))
        acc_ref[...] += dot_nt(im_ref[s], jnp.concatenate(rows, 1))
        acc_ref[:288] += dot_nt(rimz_ref[s], rows[0])
        return carry

    lax.fori_loop(0, 4, one, 0)
    acc = acc_ref[...] * (1.0 / 256)
    out_ref[...] = jnp.concatenate([acc[:432], acc[432:]], 1).astype(BF)


def finish_body(me_ref, rows_ref, f0, f1, f2, f3, first_ref, second_ref, feat_ref):
    for m, ref in enumerate((f0, f1, f2, f3)):
        feat_ref[me_ref[0] ^ m] = ref[...]
    second_ref[...] = rows_ref[:1728].astype(F32)
    packed = rows_ref[1728:2160].astype(F32)
    first_ref[:432] = packed[:, :64]
    first_ref[432:] = packed[:, 64:]


def call(body, outs, scratch=(), mib=24, final=False):
    here = pl.BlockSpec(memory_space=pltpu.VMEM)

    def run(*args):
        return pl.pallas_call(
            body,
            in_specs=[
                pl.BlockSpec(memory_space=pltpu.SMEM) if arg.shape == (1,) else here for arg in args
            ],
            out_specs=[here] * len(outs),
            out_shape=[
                jax.ShapeDtypeStruct(*out) if INTERPRET or final else pltpu.VMEM(*out) for out in outs
            ],
            scratch_shapes=list(scratch),
            compiler_params=pltpu.CompilerParams(vmem_limit_bytes=mib * 1024 * 1024),
            interpret=INTERPRET,
        )(*args)

    return run


def exchange(chunks, axis):
    return lax.all_to_all(chunks, axis, split_axis=0, concat_axis=0, tiled=True)


def reduce_stage(rows, axis):
    got = exchange(rows.reshape(lax.axis_size(axis), -1, LANES), axis)
    return jnp.sum(got.astype(F32), 0).astype(BF)


def gather_stage(rows, axis):
    copies = jnp.broadcast_to(rows[None], (lax.axis_size(axis),) + rows.shape)
    return exchange(copies, axis).reshape(-1, LANES)


def sum_everywhere(packed, wide):
    pad = jnp.zeros((144, LANES), BF)
    rows = reduce_stage(jnp.concatenate([wide, packed, pad], 0), XY_GROUP)
    got = exchange(jnp.broadcast_to(rows[None], (lax.axis_size("z"),) + rows.shape), "z")
    rows = jnp.sum(got.astype(F32), 0).astype(BF)
    return gather_stage(rows, XY_GROUP)


def swap_all(pieces):
    return [pieces[0]] + [
        lax.ppermute(pieces[m], SPACE, [(i, i ^ m) for i in range(4)]) for m in range(1, 4)
    ]


def per_device(volumes, first_kernel, second_kernel, upstream):
    table = plane_table(YD, ZD, 1)
    table2 = plane_table(YD // 2, ZD // 2, 4)
    rim = shifted(volumes[:, :, 15, :], SPACE, 1)
    me = lax.axis_index(SPACE).reshape(1)
    tile = ((128, 128), BF)
    up = upstream.reshape(128, 4, 128).transpose(1, 2, 0)
    ups = swap_all(call(pick_body, [tile] * 4)(me, up))
    w1 = first_kernel.reshape(864, 64)
    k2 = second_kernel.reshape(1728, 128)
    im1, pre1 = call(
        first_body,
        [((4, 864, 1024), BF), ((4, 64, 1024), F32)],
        scratch=[pltpu.VMEM((512, 512), BF), pltpu.VMEM((512, 1152), BF)],
    )(volumes, table, w1)
    hidden, last, slope1, rimz = call(
        rim_body,
        [((4, 64, 1024), BF), ((4, 64, 128), BF), ((4, 64, 1024), F32), ((4, 288, 128), BF)],
    )(pre1, rim, table, w1)
    halo = shifted(last, SPACE, 1)
    im2, pre2 = call(second_body, [((1728, 512), BF), ((128, 512), F32)])(hidden, table2, k2)
    *feats, delta2, edge, im2h = call(
        halo_body,
        [tile] * 4 + [((4, 128, 128), BF), tile, ((576, 512), BF)],
        scratch=[pltpu.VMEM((4, 128, 128), BF), pltpu.VMEM((4, 128, 128), BF)],
    )(me, halo, pre2, *ups, table2, k2)
    edge = shifted(edge, SPACE, -1)
    feats = swap_all(feats)
    (wide,) = call(second_grad_body, [((1728, 128), BF)])(im2, im2h, delta2)
    (packed,) = call(
        back_body,
        [((432, 128), BF)],
        scratch=[
            pltpu.VMEM((576, 256), BF),
            pltpu.VMEM((4, 256, 128), BF),
            pltpu.VMEM((864, 64), F32),
        ],
    )(delta2, edge, k2, table2, slope1, im1, rimz)
    packed, wide, *feats = lax.optimization_barrier((packed, wide, *feats))
    rows = sum_everywhere(packed, wide)
    first_grad, second_grad, features = call(
        finish_body,
        [((864, 64), F32), ((1728, 128), F32), ((4, 128, 128), BF)],
        final=True,
    )(me, rows, *feats)
    features = features.transpose(2, 0, 1).reshape(1, 128, 16, 32)
    return (features, first_grad.reshape(27, 32, 64), second_grad.reshape(27, 64, 128))


def solution(mesh):
    fine = Mesh(mesh.devices.reshape(4, 8, 2, 2, 2), ("y", "z", "xl", "xh", "c"))
    in_specs = (P(DP, None, SPACE, None), P(), P(), P(DP + SPACE, None, None, None))
    out_specs = (P(DP + SPACE, None, None, None), P(), P())
    return jax.shard_map(
        per_device, mesh=fine, in_specs=in_specs, out_specs=out_specs, check_vma=False
    )
```

```python
import jax
import jax.numpy as jnp
import numpy as np
from jax import lax
from jax.experimental import pallas as pl
from jax.experimental.pallas import tpu as pltpu
from jax.sharding import Mesh
from jax.sharding import PartitionSpec as P

YD = 32
ZD = 16
LANES = 128
DP = ("y", "z", "xl")
SPACE = ("xh", "c")
XY_GROUP = ("y", "xl", "xh", "c")
BF = jnp.bfloat16
F32 = jnp.float32
INTERPRET = False


def shifted(value, axis, steps):
    count = lax.axis_size(axis)
    initial, last = (max(0, -steps), min(count, count - steps))
    return lax.ppermute(value, axis, [(source, source + steps) for source in range(initial, last)])


def plane_table(size_y, size_z, copies):
    half_y, half_z = size_y // 2, size_z // 2
    cells = half_y * half_z
    table = np.zeros((copies, size_y * size_z, 9, copies, cells), np.float32)
    for second in range(3):
        for third in range(3):
            for out_y in range(half_y):
                for out_z in range(half_z):
                    y, z = 2 * out_y + second - 1, 2 * out_z + third - 1
                    if y >= 0 and z >= 0:
                        for k in range(copies):
                            table[k, y * size_z + z, 3 * second + third, k, out_y * half_z + out_z] = 1
    return jnp.asarray(table.reshape(copies * size_y * size_z, 9 * copies * cells), BF)


def row_order(chans, rows):
    shape = (rows * chans, chans * rows)
    at = lax.broadcasted_iota(jnp.int32, shape, 0)
    source = lax.broadcasted_iota(jnp.int32, shape, 1)
    block = at // chans
    row = (block % (rows // 2)) * 2 + block // (rows // 2)
    return (source == (at % chans) * rows + row).astype(F32).astype(BF)


def turned(value):
    size = value.shape[1]
    row = lax.broadcasted_iota(jnp.int32, (size, size), 0)
    col = lax.broadcasted_iota(jnp.int32, (size, size), 1)
    return dot_nt((row == col).astype(F32).astype(BF), value)


def dot(a, b):
    return jnp.dot(a, b, preferred_element_type=F32)


def dot_nt(a, b):
    return lax.dot_general(a, b, (((1,), (1,)), ((), ())), preferred_element_type=F32)


def act_and_slope(v):
    e = jnp.exp(-jnp.abs(v))
    act = 0.3 * v + 0.7 * (jnp.maximum(v, 0.0) + jnp.log(1.0 + e))
    slope = 0.3 + 0.7 * jnp.where(v >= 0, 1.0, e) / (1.0 + e)
    return act, slope


def first_body(
    v_hbm, table_hbm, w_hbm, im_hbm, pre_ref, wt0_ref, v_ref, table_ref, w_ref, order_ref, z_ref, im_ref, sems, v_sems, im_sems
):
    fetch_w = pltpu.make_async_copy(w_hbm, w_ref, sems.at[0])
    fetch_table = pltpu.make_async_copy(table_hbm, table_ref, sems.at[1])
    fetch_w.start()
    fetch_v = [pltpu.make_async_copy(v_hbm.at[s], v_ref.at[s], v_sems.at[s]) for s in range(4)]
    fetch_v[0].start()
    fetch_table.start()
    for s in range(1, 4):
        fetch_v[s].start()
    order_ref[...] = row_order(32, 16)
    fetch_w.wait()
    w = w_ref[...]
    below = jnp.concatenate([jnp.zeros((288, 64), BF), w[:288]], 0)
    wt = turned(jnp.concatenate([w[288:], below], 1)).astype(BF)
    wt0_ref[...] = turned(w[:288]).astype(BF)
    fetch_table.wait()

    def one(s, carry):
        pltpu.make_async_copy(v_hbm.at[s], v_ref.at[s], v_sems.at[s]).wait()
        rows = dot(order_ref[...], v_ref[s].reshape(512, 512)).astype(BF)
        z_ref[...] = dot(rows, table_ref[...]).astype(BF)
        for half in range(2):
            for o1 in range(8):
                at = (half * 8 + o1) * 32
                for t in range(9):
                    k = (9 * half + t) * 32
                    im_ref[s, k : k + 32, o1 * LANES : (o1 + 1) * LANES] = z_ref[
                        at : at + 32, t * LANES : (t + 1) * LANES
                    ]
        pltpu.make_async_copy(im_ref.at[s], im_hbm.at[s], im_sems.at[s]).start()
        got = dot(wt, im_ref[s])
        pre_ref[s, :, :LANES] = got[:64, :LANES]
        pre_ref[s, :, LANES:] = got[:64, LANES:] + got[64:, :-LANES]
        return carry

    lax.fori_loop(0, 4, one, 0)
    for s in range(4):
        pltpu.make_async_copy(im_ref.at[s], im_hbm.at[s], im_sems.at[s]).wait()


def rim_body(
    me_ref, up_hbm, pre_ref, rim_ref, table_ref, wt0_ref, hid_ref, send_ref, send2, send3, own_ref, slope_ref, rimz_ref, up_ref, sem
):
    fetch = pltpu.make_async_copy(up_hbm, up_ref, sem)
    fetch.start()
    z = dot(rim_ref[...].reshape(128, 512), table_ref[...]).astype(BF)
    for s in range(4):
        im = jnp.concatenate(
            [z[32 * s : 32 * s + 32, t * LANES : (t + 1) * LANES] for t in range(9)], 0
        )
        rimz_ref[s] = im
        extra = dot(wt0_ref[...], im)
        for r in range(8):
            lanes = slice(r * LANES, (r + 1) * LANES)
            pre = pre_ref[s, :, lanes]
            if r == 0:
                pre = pre + extra
            act, slope = act_and_slope(pre)
            hidden = act.astype(BF)
            hid_ref[s, :, lanes] = hidden
            slope_ref[s, :, lanes] = slope
            if r == 7:
                send_ref[64 * s : 64 * s + 64] = hidden
    fetch.wait()
    me = me_ref[0]
    send_ref[256:] = up_ref[(me + 1) & 3]
    send2[...] = up_ref[(me + 2) & 3]
    send3[...] = up_ref[(me + 3) & 3]
    own_ref[...] = up_ref[me]


def second_body(hid_ref, table_ref, w_ref, im_ref, pre_ref):
    for s in range(4):
        row = lambda r: (
            hid_ref[s, :, r * LANES : (r + 1) * LANES] if r >= 0 else jnp.zeros((64, LANES), BF)
        )
        left = jnp.concatenate(
            [jnp.concatenate([row(2 * o1 + a - 1) for o1 in range(4)], 1) for a in range(3)], 0
        )
        z = dot(left, table_ref[...]).astype(BF)
        for a in range(3):
            for t in range(9):
                k = (9 * a + t) * 64
                im_ref[k : k + 64, s * LANES : (s + 1) * LANES] = z[
                    64 * a : 64 * a + 64, t * LANES : (t + 1) * LANES
                ]
    pre_ref[...] = dot(turned(w_ref[...]).astype(BF), im_ref[...])


def halo_body(me_ref, got_ref, pre_ref, own_ref, got2, got3, table_ref, w_ref, *refs):
    send_ref, send2, send3, kept_ref, delta_ref, imh_ref, up_ref, feat_ref = refs
    me = me_ref[0]
    up_ref[me] = own_ref[...]
    up_ref[(me + 1) & 3] = got3[...]
    up_ref[(me + 2) & 3] = got2[...]
    up_ref[(me + 3) & 3] = got_ref[256:]
    z = dot(got_ref[:256], table_ref[:LANES, :])
    z = jnp.where(me > 0, z, 0.0).astype(BF)
    for s in range(4):
        for t in range(9):
            imh_ref[t * 64 : t * 64 + 64, s * LANES : (s + 1) * LANES] = z[
                64 * s : 64 * s + 64, t * LANES : (t + 1) * LANES
            ]
    pre = pre_ref[...] + dot(turned(w_ref[:576]).astype(BF), imh_ref[...])
    lane = lax.broadcasted_iota(jnp.int32, (128, LANES), 1)
    edge = jnp.zeros((128, LANES), F32)
    for s in range(4):
        act, slope = act_and_slope(pre[:, s * LANES : (s + 1) * LANES])
        feat_ref[s] = turned(act.astype(BF)).astype(BF)
        delta = (turned(up_ref[s]) * slope).astype(BF)
        delta_ref[s] = delta
        moved = delta.astype(F32)
        if s:
            moved = pltpu.roll(moved, 32 * s, 1)
        edge = jnp.where(lane // 32 == s, moved, edge)
    send_ref[:128] = edge.astype(BF)
    send_ref[128:] = feat_ref[(me + 3) & 3]
    send2[...] = feat_ref[(me + 2) & 3]
    send3[...] = feat_ref[(me + 1) & 3]
    kept_ref[...] = feat_ref[me]


def second_grad_body(im_ref, imh_ref, delta_ref, out_ref):
    scale = 1.0 / 256
    delta = jnp.concatenate([delta_ref[s] for s in range(4)], 1)
    out_ref[:576] = (dot_nt(im_ref[:576] + imh_ref[...], delta) * scale).astype(BF)
    out_ref[576:] = (dot_nt(im_ref[576:], delta) * scale).astype(BF)


def back_body(
    me_ref, im_hbm, wide_ref, delta_ref, got_ref, k_ref, table_ref, slope_ref, rimz_ref, out_ref, kodd_ref, ahead_ref, acc_ref, im_ref, sems
):
    for s in range(4):
        pltpu.make_async_copy(im_hbm.at[s], im_ref.at[s], sems.at[s]).start()
    lane = lax.broadcasted_iota(jnp.int32, (128, LANES), 1)
    acc_ref[...] = jnp.zeros_like(acc_ref)
    kodd_ref[:, :128] = k_ref[:576]
    kodd_ref[:, 128:] = k_ref[1152:]
    rim = jnp.where(me_ref[0] < 3, got_ref[:128].astype(F32), 0.0)
    for s in range(4):
        own = delta_ref[s]
        moved = pltpu.roll(own.astype(F32), 96, 1)
        ends = pltpu.roll(rim, 96 - 32 * s, 1) if s != 3 else rim
        ahead_ref[s, :128] = jnp.where(lane < 96, moved, ends).astype(BF)
        ahead_ref[s, 128:] = own

    def one(s, carry):
        even = dot(k_ref[576:1152], delta_ref[s])
        odd = dot(kodd_ref[...], ahead_ref[s])
        parts = []
        for grad in (even, odd):
            flat = jnp.concatenate([grad[64 * t : 64 * t + 64] for t in range(9)], 1)
            high = flat.astype(BF)
            parts += [high, (flat - high.astype(F32)).astype(BF)]
        got = dot_nt(jnp.concatenate(parts, 0), table_ref[...])
        rows = []
        for r in range(8):
            base = 128 * (r % 2)
            lanes = slice((r // 2) * LANES, (r // 2 + 1) * LANES)
            back = (got[base : base + 64, lanes] + got[base + 64 : base + 128, lanes]).astype(BF)
            slope = slope_ref[s, :, r * LANES : (r + 1) * LANES]
            rows.append((back.astype(F32) * slope).astype(BF))
        zero = jnp.zeros((64, LANES), BF)
        both = jnp.concatenate(
            [jnp.concatenate(rows, 1), jnp.concatenate(rows[1:] + [zero], 1)], 0
        )
        pltpu.make_async_copy(im_hbm.at[s], im_ref.at[s], sems.at[s]).wait()
        acc_ref[...] += dot_nt(im_ref[s], both)
        acc_ref[288:] += dot_nt(rimz_ref[s], jnp.concatenate([zero, rows[0]], 0))
        return carry

    lax.fori_loop(0, 4, one, 0)
    acc = acc_ref[...] * (1.0 / 256)
    out_ref[:1728] = wide_ref[...]
    out_ref[2160:] = jnp.zeros((144, LANES), BF)
    out_ref[1728:2016] = acc[288:].astype(BF)
    out_ref[2016:2160] = jnp.concatenate([acc[:144, :64], acc[144:288, :64]], 1).astype(BF)


def finish_body(me_ref, rows_ref, kept_ref, got_ref, got2, got3, first_ref, second_ref, feat_ref):
    me = me_ref[0]
    feat_ref[me] = kept_ref[...]
    feat_ref[(me + 1) & 3] = got_ref[128:]
    feat_ref[(me + 2) & 3] = got2[...]
    feat_ref[(me + 3) & 3] = got3[...]
    second_ref[...] = rows_ref[:1728].astype(F32)
    odd = rows_ref[1728:2016].astype(F32)
    even = rows_ref[2016:2160].astype(F32)
    first_ref[:288] = odd[:, 64:]
    first_ref[288:432] = even[:, :64]
    first_ref[432:576] = even[:, 64:]
    first_ref[576:] = odd[:, :64]


def call(body, outs, scratch=(), mib=24, final=False, far=(), far_outs=()):
    here = pl.BlockSpec(memory_space=pltpu.VMEM)
    there = pl.BlockSpec(memory_space=pl.ANY if INTERPRET else pltpu.HBM)
    scalar = pl.BlockSpec(memory_space=pltpu.SMEM)

    def shape_of(at, out):
        if INTERPRET or final:
            return jax.ShapeDtypeStruct(*out)
        return pltpu.HBM(*out) if at in far_outs else pltpu.VMEM(*out)

    def run(*args):
        if not INTERPRET:
            args = [
                pltpu.with_memory_space_constraint(arg, pltpu.HBM) if at in far else arg
                for at, arg in enumerate(args)
            ]
        return pl.pallas_call(
            body,
            in_specs=[
                scalar if arg.shape == (1,) else there if at in far else here
                for at, arg in enumerate(args)
            ],
            out_specs=[there if at in far_outs else here for at in range(len(outs))],
            out_shape=[shape_of(at, out) for at, out in enumerate(outs)],
            scratch_shapes=list(scratch),
            compiler_params=pltpu.CompilerParams(vmem_limit_bytes=mib * 1024 * 1024),
            interpret=INTERPRET,
        )(*args)

    return run


def exchange(chunks, axis):
    return lax.all_to_all(chunks, axis, split_axis=0, concat_axis=0, tiled=True)


def reduce_stage(rows, axis):
    got = exchange(rows.reshape(lax.axis_size(axis), -1, LANES), axis)
    return jnp.sum(got.astype(F32), 0).astype(BF)


def gather_stage(rows, axis):
    copies = jnp.broadcast_to(rows[None], (lax.axis_size(axis),) + rows.shape)
    return exchange(copies, axis).reshape(-1, LANES)


def sum_everywhere(rows):
    rows = reduce_stage(rows, XY_GROUP)
    got = exchange(jnp.broadcast_to(rows[None], (lax.axis_size("z"),) + rows.shape), "z")
    rows = jnp.sum(got.astype(F32), 0).astype(BF)
    return gather_stage(rows, XY_GROUP)


def rotated(value, steps):
    return lax.ppermute(value, SPACE, [(i, (i + steps) % 4) for i in range(4)])


def per_device(volumes, first_kernel, second_kernel, upstream):
    table = plane_table(YD, ZD, 1)
    table2 = plane_table(YD // 2, ZD // 2, 4)
    rim = shifted(volumes[:, :, 15, :], SPACE, 1)
    me = lax.axis_index(SPACE).reshape(1)
    tile = ((128, 128), BF)
    up = upstream.reshape(128, 4, 128).transpose(1, 2, 0)
    w1 = first_kernel.reshape(864, 64)
    k2 = second_kernel.reshape(1728, 128)
    im1, pre1, wt0 = call(
        first_body,
        [((4, 576, 1024), BF), ((4, 64, 1024), F32), ((64, 288), BF)],
        scratch=[
            pltpu.VMEM((4, 32, 16, 512), BF),
            pltpu.VMEM((512, 1152), BF),
            pltpu.VMEM((864, 64), BF),
            pltpu.VMEM((512, 512), BF),
            pltpu.VMEM((512, 1152), BF),
            pltpu.VMEM((4, 576, 1024), BF),
            pltpu.SemaphoreType.DMA((2,)),
            pltpu.SemaphoreType.DMA((4,)),
            pltpu.SemaphoreType.DMA((4,)),
        ],
        far=(0, 1, 2),
        far_outs=(0,),
    )(volumes, table, w1)
    hidden, sent, sent2, sent3, own, slope1, rimz = call(
        rim_body,
        [
            ((4, 64, 1024), BF),
            ((384, 128), BF),
            tile,
            tile,
            tile,
            ((4, 64, 1024), F32),
            ((4, 288, 128), BF),
        ],
        scratch=[pltpu.VMEM((4, 128, 128), BF), pltpu.SemaphoreType.DMA(())],
        far=(1,),
    )(me, up, pre1, rim, table, wt0)
    got = rotated(sent, 1)
    got2 = rotated(sent2, 2)
    got3 = rotated(sent3, 3)
    im2, pre2 = call(second_body, [((1728, 512), BF), ((128, 512), F32)])(hidden, table2, k2)
    sent, sent2, sent3, kept, delta2, im2h = call(
        halo_body,
        [((256, 128), BF), tile, tile, tile, ((4, 128, 128), BF), ((576, 512), BF)],
        scratch=[pltpu.VMEM((4, 128, 128), BF), pltpu.VMEM((4, 128, 128), BF)],
    )(me, got, pre2, own, got2, got3, table2, k2)
    got = rotated(sent, 3)
    got2 = rotated(sent2, 2)
    got3 = rotated(sent3, 1)
    (wide,) = call(second_grad_body, [((1728, 128), BF)])(im2, im2h, delta2)
    (rows,) = call(
        back_body,
        [((2304, 128), BF)],
        scratch=[
            pltpu.VMEM((576, 256), BF),
            pltpu.VMEM((4, 256, 128), BF),
            pltpu.VMEM((576, 128), F32),
            pltpu.VMEM((4, 576, 1024), BF),
            pltpu.SemaphoreType.DMA((4,)),
        ],
        far=(1,),
    )(me, im1, wide, delta2, got, k2, table2, slope1, rimz)
    rows, got2, got3 = lax.optimization_barrier((rows, got2, got3))
    rows = sum_everywhere(rows)
    first_grad, second_grad, features = call(
        finish_body,
        [((864, 64), F32), ((1728, 128), F32), ((4, 128, 128), BF)],
        final=True,
    )(me, rows, kept, got, got2, got3)
    features = features.transpose(2, 0, 1).reshape(1, 128, 16, 32)
    return (features, first_grad.reshape(27, 32, 64), second_grad.reshape(27, 64, 128))


def solution(mesh):
    fine = Mesh(mesh.devices.reshape(4, 8, 2, 2, 2), ("y", "z", "xl", "xh", "c"))
    in_specs = (P(DP, None, SPACE, None), P(), P(), P(DP + SPACE, None, None, None))
    out_specs = (P(DP + SPACE, None, None, None), P(), P())
    return jax.shard_map(
        per_device, mesh=fine, in_specs=in_specs, out_specs=out_specs, check_vma=False
    )
```

```python
import jax
import jax.numpy as jnp
import numpy as np
from jax import lax
from jax.experimental import pallas as pl
from jax.experimental.pallas import tpu as pltpu
from jax.sharding import Mesh
from jax.sharding import PartitionSpec as P

YD = 32
ZD = 16
LANES = 128
DP = ("y", "z", "xl")
SPACE = ("xh", "c")
XY_GROUP = ("y", "xl", "xh", "c")
BF = jnp.bfloat16
F32 = jnp.float32
INTERPRET = False


def shifted(value, axis, steps):
    count = lax.axis_size(axis)
    initial, last = (max(0, -steps), min(count, count - steps))
    return lax.ppermute(value, axis, [(source, source + steps) for source in range(initial, last)])


def phase_table(size_y, size_z, copies):
    shape = (copies, size_y // 2, 2, size_z // 2, 2)
    at = np.arange(np.prod(shape)).reshape(shape).transpose(2, 4, 0, 1, 3).reshape(-1)
    return jnp.asarray(np.eye(at.size, dtype=np.float32)[:, at], BF)


def tap_masks(shape, row, cells):
    lane = lax.broadcasted_iota(jnp.int32, shape, 1) % cells
    return lane >= row, lane % row != 0


def tap_parts(row):
    for second in range(3):
        for third in range(3):
            back_y, back_z = second == 0, third == 0
            yield 2 * (second != 1) + (third != 1), row * back_y + back_z, back_y, back_z


def spread(phases, row, cells):
    in_y, in_z = tap_masks((phases.shape[0], LANES), row, cells)
    taps = []
    for phase, steps, back_y, back_z in tap_parts(row):
        tap = phases[:, phase * LANES : (phase + 1) * LANES]
        if steps:
            mask = in_y & in_z if back_y and back_z else in_y if back_y else in_z
            tap = jnp.where(mask, pltpu.roll(tap, steps, 1), 0.0)
        taps.append(tap)
    return taps


def collect(taps, row, cells):
    in_y, in_z = tap_masks(taps[0].shape, row, cells)
    phases = [None] * 4
    for tap, (phase, steps, back_y, back_z) in zip(taps, tap_parts(row)):
        if steps:
            mask = in_y & in_z if back_y and back_z else in_y if back_y else in_z
            tap = pltpu.roll(jnp.where(mask, tap, 0.0), LANES - steps, 1)
        phases[phase] = tap if phases[phase] is None else phases[phase] + tap
    return jnp.concatenate(phases, 1)


def row_order(chans, rows):
    shape = (rows * chans, chans * rows)
    at = lax.broadcasted_iota(jnp.int32, shape, 0)
    source = lax.broadcasted_iota(jnp.int32, shape, 1)
    block = at // chans
    row = (block % (rows // 2)) * 2 + block // (rows // 2)
    return (source == (at % chans) * rows + row).astype(F32).astype(BF)


def turned(value):
    size = value.shape[1]
    row = lax.broadcasted_iota(jnp.int32, (size, size), 0)
    col = lax.broadcasted_iota(jnp.int32, (size, size), 1)
    return dot_nt((row == col).astype(F32).astype(BF), value)


def dot(a, b):
    return jnp.dot(a, b, preferred_element_type=F32)


def dot_nt(a, b):
    return lax.dot_general(a, b, (((1,), (1,)), ((), ())), preferred_element_type=F32)


def act_and_slope(v):
    e = jnp.exp(-jnp.abs(v))
    act = 0.3 * v + 0.7 * (jnp.maximum(v, 0.0) + jnp.log(1.0 + e))
    slope = 0.3 + 0.7 * jnp.where(v >= 0, 1.0, e) / (1.0 + e)
    return act, slope


def load_body(
    v_hbm, w_hbm, table_hbm, rows_ref, rim_ref, wt_ref, wt0_ref, table_ref, v_ref, w_ref, sems, v_sems
):
    fetch_w = pltpu.make_async_copy(w_hbm, w_ref, sems.at[0])
    fetch_table = pltpu.make_async_copy(table_hbm, table_ref, sems.at[1])
    fetch_v = [pltpu.make_async_copy(v_hbm.at[s], v_ref.at[s], v_sems.at[s]) for s in range(4)]
    for fetch in [fetch_w] + fetch_v + [fetch_table]:
        fetch.start()
    order = row_order(32, 16)
    fetch_w.wait()
    w = w_ref[...]
    below = jnp.concatenate([jnp.zeros((288, 64), BF), w[:288]], 0)
    wt_ref[...] = turned(jnp.concatenate([w[288:], below], 1)).astype(BF)
    wt0_ref[...] = turned(w[:288]).astype(BF)
    for s in range(4):
        fetch_v[s].wait()
        rows = dot(order, v_ref[s].reshape(512, 512)).astype(BF)
        rows_ref[s] = rows
        rim_ref[s] = rows[480:]
    fetch_table.wait()


def first_body(rows_ref, table_ref, wt_ref, im_hbm, pre_ref, z_ref, im_ref, im_sems):
    def one(s, carry):
        z_ref[...] = dot(rows_ref[s], table_ref[...])
        for half in range(2):
            for o1 in range(8):
                at = (half * 8 + o1) * 32
                for t, tap in enumerate(spread(z_ref[at : at + 32], 8, 128)):
                    k = (9 * half + t) * 32
                    im_ref[s, k : k + 32, o1 * LANES : (o1 + 1) * LANES] = tap.astype(BF)
        pltpu.make_async_copy(im_ref.at[s], im_hbm.at[s], im_sems.at[s]).start()
        got = dot(wt_ref[...], im_ref[s])
        pre_ref[s, :, :LANES] = got[:64, :LANES]
        pre_ref[s, :, LANES:] = got[:64, LANES:] + got[64:, :-LANES]
        return carry

    lax.fori_loop(0, 4, one, 0)
    for s in range(4):
        pltpu.make_async_copy(im_ref.at[s], im_hbm.at[s], im_sems.at[s]).wait()


def rim_body(
    me_ref, up_hbm, pre_ref, rim_ref, table_ref, wt0_ref, hid_ref, send_ref, send2, send3, own_ref, slope_ref, rimz_ref, up_ref, sem
):
    fetch = pltpu.make_async_copy(up_hbm, up_ref, sem)
    fetch.start()
    taps = spread(dot(rim_ref[...].reshape(128, 512), table_ref[...]), 8, 128)
    for s in range(4):
        im = jnp.concatenate([tap[32 * s : 32 * s + 32] for tap in taps], 0).astype(BF)
        rimz_ref[s] = im
        extra = dot(wt0_ref[...], im)
        for r in range(8):
            lanes = slice(r * LANES, (r + 1) * LANES)
            pre = pre_ref[s, :, lanes]
            if r == 0:
                pre = pre + extra
            act, slope = act_and_slope(pre)
            hidden = act.astype(BF)
            hid_ref[s, :, lanes] = hidden
            slope_ref[s, :, lanes] = slope
            if r == 7:
                send_ref[64 * s : 64 * s + 64] = hidden
    fetch.wait()
    me = me_ref[0]
    send_ref[256:] = up_ref[(me + 1) & 3]
    send2[...] = up_ref[(me + 2) & 3]
    send3[...] = up_ref[(me + 3) & 3]
    own_ref[...] = up_ref[me]


def second_body(hid_ref, table_ref, w_ref, im_ref, pre_ref):
    for s in range(4):
        row = lambda r: (
            hid_ref[s, :, r * LANES : (r + 1) * LANES] if r >= 0 else jnp.zeros((64, LANES), BF)
        )
        left = jnp.concatenate(
            [jnp.concatenate([row(2 * o1 + a - 1) for o1 in range(4)], 1) for a in range(3)], 0
        )
        for t, tap in enumerate(spread(dot(left, table_ref[...]), 4, 32)):
            for a in range(3):
                k = (9 * a + t) * 64
                im_ref[k : k + 64, s * LANES : (s + 1) * LANES] = tap[
                    64 * a : 64 * a + 64
                ].astype(BF)
    pre_ref[...] = dot(turned(w_ref[...]).astype(BF), im_ref[...])


def halo_body(me_ref, got_ref, pre_ref, own_ref, got2, got3, table_ref, w_ref, *refs):
    send_ref, send2, send3, kept_ref, delta_ref, imh_ref, up_ref, feat_ref = refs
    me = me_ref[0]
    up_ref[me] = own_ref[...]
    up_ref[(me + 1) & 3] = got3[...]
    up_ref[(me + 2) & 3] = got2[...]
    up_ref[(me + 3) & 3] = got_ref[256:]
    z = dot(got_ref[:256], table_ref[:LANES, :])
    for t, tap in enumerate(spread(jnp.where(me > 0, z, 0.0), 4, 32)):
        for s in range(4):
            imh_ref[t * 64 : t * 64 + 64, s * LANES : (s + 1) * LANES] = tap[
                64 * s : 64 * s + 64
            ].astype(BF)
    pre = pre_ref[...] + dot(turned(w_ref[:576]).astype(BF), imh_ref[...])
    lane = lax.broadcasted_iota(jnp.int32, (128, LANES), 1)
    edge = jnp.zeros((128, LANES), F32)
    for s in range(4):
        act, slope = act_and_slope(pre[:, s * LANES : (s + 1) * LANES])
        feat_ref[s] = turned(act.astype(BF)).astype(BF)
        delta = (turned(up_ref[s]) * slope).astype(BF)
        delta_ref[s] = delta
        moved = delta.astype(F32)
        if s:
            moved = pltpu.roll(moved, 32 * s, 1)
        edge = jnp.where(lane // 32 == s, moved, edge)
    send_ref[:128] = edge.astype(BF)
    send_ref[128:] = feat_ref[(me + 3) & 3]
    send2[...] = feat_ref[(me + 2) & 3]
    send3[...] = feat_ref[(me + 1) & 3]
    kept_ref[...] = feat_ref[me]


def second_grad_body(im_ref, imh_ref, delta_ref, out_ref):
    scale = 1.0 / 256
    delta = jnp.concatenate([delta_ref[s] for s in range(4)], 1)
    out_ref[:576] = (dot_nt(im_ref[:576] + imh_ref[...], delta) * scale).astype(BF)
    out_ref[576:] = (dot_nt(im_ref[576:], delta) * scale).astype(BF)


def back_body(
    me_ref, im_hbm, wide_ref, delta_ref, got_ref, k_ref, table_ref, slope_ref, rimz_ref, out_ref, kodd_ref, ahead_ref, acc_ref, im_ref, sems
):
    for s in range(4):
        pltpu.make_async_copy(im_hbm.at[s], im_ref.at[s], sems.at[s]).start()
    lane = lax.broadcasted_iota(jnp.int32, (128, LANES), 1)
    acc_ref[...] = jnp.zeros_like(acc_ref)
    kodd_ref[:, :128] = k_ref[:576]
    kodd_ref[:, 128:] = k_ref[1152:]
    rim = jnp.where(me_ref[0] < 3, got_ref[:128].astype(F32), 0.0)
    for s in range(4):
        own = delta_ref[s]
        moved = pltpu.roll(own.astype(F32), 96, 1)
        ends = pltpu.roll(rim, 96 - 32 * s, 1) if s != 3 else rim
        ahead_ref[s, :128] = jnp.where(lane < 96, moved, ends).astype(BF)
        ahead_ref[s, 128:] = own

    def one(s, carry):
        even = dot(k_ref[576:1152], delta_ref[s])
        odd = dot(kodd_ref[...], ahead_ref[s])
        parts = []
        for grad in (even, odd):
            flat = collect([grad[64 * t : 64 * t + 64] for t in range(9)], 4, 32)
            high = flat.astype(BF)
            parts += [high, (flat - high.astype(F32)).astype(BF)]
        got = dot_nt(jnp.concatenate(parts, 0), table_ref[...])
        rows = []
        for r in range(8):
            base = 128 * (r % 2)
            lanes = slice((r // 2) * LANES, (r // 2 + 1) * LANES)
            back = (got[base : base + 64, lanes] + got[base + 64 : base + 128, lanes]).astype(BF)
            slope = slope_ref[s, :, r * LANES : (r + 1) * LANES]
            rows.append((back.astype(F32) * slope).astype(BF))
        zero = jnp.zeros((64, LANES), BF)
        both = jnp.concatenate(
            [jnp.concatenate(rows, 1), jnp.concatenate(rows[1:] + [zero], 1)], 0
        )
        pltpu.make_async_copy(im_hbm.at[s], im_ref.at[s], sems.at[s]).wait()
        acc_ref[...] += dot_nt(im_ref[s], both)
        acc_ref[288:] += dot_nt(rimz_ref[s], jnp.concatenate([zero, rows[0]], 0))
        return carry

    lax.fori_loop(0, 4, one, 0)
    acc = acc_ref[...] * (1.0 / 256)
    out_ref[:1728] = wide_ref[...]
    out_ref[2160:] = jnp.zeros((144, LANES), BF)
    out_ref[1728:2016] = acc[288:].astype(BF)
    out_ref[2016:2160] = jnp.concatenate([acc[:144, :64], acc[144:288, :64]], 1).astype(BF)


def finish_body(me_ref, rows_ref, kept_ref, got_ref, got2, got3, first_ref, second_ref, feat_ref):
    me = me_ref[0]
    feat_ref[me] = kept_ref[...]
    feat_ref[(me + 1) & 3] = got_ref[128:]
    feat_ref[(me + 2) & 3] = got2[...]
    feat_ref[(me + 3) & 3] = got3[...]
    second_ref[...] = rows_ref[:1728].astype(F32)
    odd = rows_ref[1728:2016].astype(F32)
    even = rows_ref[2016:2160].astype(F32)
    first_ref[:288] = odd[:, 64:]
    first_ref[288:432] = even[:, :64]
    first_ref[432:576] = even[:, 64:]
    first_ref[576:] = odd[:, :64]


def call(body, outs, scratch=(), mib=24, final=False, far=(), far_outs=()):
    here = pl.BlockSpec(memory_space=pltpu.VMEM)
    there = pl.BlockSpec(memory_space=pl.ANY if INTERPRET else pltpu.HBM)
    scalar = pl.BlockSpec(memory_space=pltpu.SMEM)

    def shape_of(at, out):
        if INTERPRET or final:
            return jax.ShapeDtypeStruct(*out)
        return pltpu.HBM(*out) if at in far_outs else pltpu.VMEM(*out)

    def run(*args):
        if not INTERPRET:
            args = [
                pltpu.with_memory_space_constraint(arg, pltpu.HBM) if at in far else arg
                for at, arg in enumerate(args)
            ]
        return pl.pallas_call(
            body,
            in_specs=[
                scalar if arg.shape == (1,) else there if at in far else here
                for at, arg in enumerate(args)
            ],
            out_specs=[there if at in far_outs else here for at in range(len(outs))],
            out_shape=[shape_of(at, out) for at, out in enumerate(outs)],
            scratch_shapes=list(scratch),
            compiler_params=pltpu.CompilerParams(vmem_limit_bytes=mib * 1024 * 1024),
            interpret=INTERPRET,
        )(*args)

    return run


def exchange(chunks, axis):
    return lax.all_to_all(chunks, axis, split_axis=0, concat_axis=0, tiled=True)


def reduce_stage(rows, axis):
    got = exchange(rows.reshape(lax.axis_size(axis), -1, LANES), axis)
    return jnp.sum(got.astype(F32), 0).astype(BF)


def gather_stage(rows, axis):
    copies = jnp.broadcast_to(rows[None], (lax.axis_size(axis),) + rows.shape)
    return exchange(copies, axis).reshape(-1, LANES)


def sum_everywhere(rows):
    rows = reduce_stage(rows, XY_GROUP)
    got = exchange(jnp.broadcast_to(rows[None], (lax.axis_size("z"),) + rows.shape), "z")
    rows = jnp.sum(got.astype(F32), 0).astype(BF)
    return gather_stage(rows, XY_GROUP)


def rotated(value, steps):
    return lax.ppermute(value, SPACE, [(i, (i + steps) % 4) for i in range(4)])


def per_device(volumes, first_kernel, second_kernel, upstream):
    me = lax.axis_index(SPACE).reshape(1)
    tile = ((128, 128), BF)
    table = phase_table(YD, ZD, 1)
    table2 = phase_table(YD // 2, ZD // 2, 4)
    k2 = second_kernel.reshape(1728, 128)
    up = upstream.reshape(128, 4, 128).transpose(1, 2, 0)
    rows, rim, wt, wt0, near_table = call(
        load_body,
        [
            ((4, 512, 512), BF),
            ((4, 32, 512), BF),
            ((128, 576), BF),
            ((64, 288), BF),
            ((512, 512), BF),
        ],
        scratch=[
            pltpu.VMEM((4, 32, 16, 512), BF),
            pltpu.VMEM((864, 64), BF),
            pltpu.SemaphoreType.DMA((2,)),
            pltpu.SemaphoreType.DMA((4,)),
        ],
        far=(0, 1, 2),
    )(volumes, first_kernel.reshape(864, 64), table)
    rim = shifted(rim, SPACE, 1)
    im1, pre1 = call(
        first_body,
        [((4, 576, 1024), BF), ((4, 64, 1024), F32)],
        scratch=[
            pltpu.VMEM((512, 512), F32),
            pltpu.VMEM((4, 576, 1024), BF),
            pltpu.SemaphoreType.DMA((4,)),
        ],
        far_outs=(0,),
    )(rows, near_table, wt)
    hidden, sent, sent2, sent3, own, slope1, rimz = call(
        rim_body,
        [
            ((4, 64, 1024), BF),
            ((384, 128), BF),
            tile,
            tile,
            tile,
            ((4, 64, 1024), F32),
            ((4, 288, 128), BF),
        ],
        scratch=[pltpu.VMEM((4, 128, 128), BF), pltpu.SemaphoreType.DMA(())],
        far=(1,),
    )(me, up, pre1, rim, table, wt0)
    got = rotated(sent, 1)
    got2 = rotated(sent2, 2)
    got3 = rotated(sent3, 3)
    im2, pre2 = call(second_body, [((1728, 512), BF), ((128, 512), F32)])(hidden, table2, k2)
    sent, sent2, sent3, kept, delta2, im2h = call(
        halo_body,
        [((256, 128), BF), tile, tile, tile, ((4, 128, 128), BF), ((576, 512), BF)],
        scratch=[pltpu.VMEM((4, 128, 128), BF), pltpu.VMEM((4, 128, 128), BF)],
    )(me, got, pre2, own, got2, got3, table2, k2)
    got = rotated(sent, 3)
    got2 = rotated(sent2, 2)
    got3 = rotated(sent3, 1)
    (wide,) = call(second_grad_body, [((1728, 128), BF)])(im2, im2h, delta2)
    (rows,) = call(
        back_body,
        [((2304, 128), BF)],
        scratch=[
            pltpu.VMEM((576, 256), BF),
            pltpu.VMEM((4, 256, 128), BF),
            pltpu.VMEM((576, 128), F32),
            pltpu.VMEM((4, 576, 1024), BF),
            pltpu.SemaphoreType.DMA((4,)),
        ],
        far=(1,),
    )(me, im1, wide, delta2, got, k2, table2, slope1, rimz)
    rows, got2, got3 = lax.optimization_barrier((rows, got2, got3))
    rows = sum_everywhere(rows)
    first_grad, second_grad, features = call(
        finish_body,
        [((864, 64), F32), ((1728, 128), F32), ((4, 128, 128), BF)],
        final=True,
    )(me, rows, kept, got, got2, got3)
    features = features.transpose(2, 0, 1).reshape(1, 128, 16, 32)
    return (features, first_grad.reshape(27, 32, 64), second_grad.reshape(27, 64, 128))


def solution(mesh):
    fine = Mesh(mesh.devices.reshape(4, 8, 2, 2, 2), ("y", "z", "xl", "xh", "c"))
    in_specs = (P(DP, None, SPACE, None), P(), P(), P(DP + SPACE, None, None, None))
    out_specs = (P(DP + SPACE, None, None, None), P(), P())
    return jax.shard_map(
        per_device, mesh=fine, in_specs=in_specs, out_specs=out_specs, check_vma=False
    )
```

```python
import jax
import jax.numpy as jnp
import numpy as np
from jax import lax
from jax.experimental import pallas as pl
from jax.experimental.pallas import tpu as pltpu
from jax.sharding import Mesh
from jax.sharding import PartitionSpec as P

YD = 32
ZD = 16
LANES = 128
DP = ("y", "z", "xl")
SPACE = ("xh", "c")
XY_GROUP = ("y", "xl", "xh")
BF = jnp.bfloat16
F32 = jnp.float32
INTERPRET = False


def shifted(value, axis, steps):
    count = lax.axis_size(axis)
    initial, last = (max(0, -steps), min(count, count - steps))
    return lax.ppermute(value, axis, [(source, source + steps) for source in range(initial, last)])


def phase_table(size_y, size_z, copies):
    shape = (copies, size_y // 2, 2, size_z // 2, 2)
    at = np.arange(np.prod(shape)).reshape(shape).transpose(2, 4, 0, 1, 3).reshape(-1)
    return jnp.asarray(np.eye(at.size, dtype=np.float32)[:, at], BF)


def tap_masks(shape, row, cells):
    lane = lax.broadcasted_iota(jnp.int32, shape, 1) % cells
    return lane >= row, lane % row != 0


def tap_parts(row):
    for second in range(3):
        for third in range(3):
            back_y, back_z = second == 0, third == 0
            yield 2 * (second != 1) + (third != 1), row * back_y + back_z, back_y, back_z


def spread(phases, row, cells):
    in_y, in_z = tap_masks((phases.shape[0], LANES), row, cells)
    taps = []
    for phase, steps, back_y, back_z in tap_parts(row):
        tap = phases[:, phase * LANES : (phase + 1) * LANES]
        if steps:
            mask = in_y & in_z if back_y and back_z else in_y if back_y else in_z
            tap = jnp.where(mask, pltpu.roll(tap, steps, 1), 0.0)
        taps.append(tap)
    return taps


def collect(taps, row, cells):
    in_y, in_z = tap_masks(taps[0].shape, row, cells)
    phases = [None] * 4
    for tap, (phase, steps, back_y, back_z) in zip(taps, tap_parts(row)):
        if steps:
            mask = in_y & in_z if back_y and back_z else in_y if back_y else in_z
            tap = pltpu.roll(jnp.where(mask, tap, 0.0), LANES - steps, 1)
        phases[phase] = tap if phases[phase] is None else phases[phase] + tap
    return jnp.concatenate(phases, 1)


def row_order(chans, rows):
    shape = (rows * chans, chans * rows)
    at = lax.broadcasted_iota(jnp.int32, shape, 0)
    source = lax.broadcasted_iota(jnp.int32, shape, 1)
    block = at // chans
    row = (block % (rows // 2)) * 2 + block // (rows // 2)
    return (source == (at % chans) * rows + row).astype(F32).astype(BF)


def turned(value):
    size = value.shape[1]
    row = lax.broadcasted_iota(jnp.int32, (size, size), 0)
    col = lax.broadcasted_iota(jnp.int32, (size, size), 1)
    return dot_nt((row == col).astype(F32).astype(BF), value)


def dot(a, b):
    return jnp.dot(a, b, preferred_element_type=F32)


def dot_nt(a, b):
    return lax.dot_general(a, b, (((1,), (1,)), ((), ())), preferred_element_type=F32)


def act_and_slope(v):
    e = jnp.exp(-jnp.abs(v))
    act = 0.3 * v + 0.7 * (jnp.maximum(v, 0.0) + jnp.log(1.0 + e))
    slope = 0.3 + 0.7 * jnp.where(v >= 0, 1.0, e) / (1.0 + e)
    return act, slope


def load_body(
    v_hbm, w_hbm, table_hbm, rows_ref, rim_ref, wt_ref, wt0_ref, table_ref, v_ref, w_ref, sems, v_sems
):
    fetch_w = pltpu.make_async_copy(w_hbm, w_ref, sems.at[0])
    fetch_table = pltpu.make_async_copy(table_hbm, table_ref, sems.at[1])
    fetch_v = [pltpu.make_async_copy(v_hbm.at[s], v_ref.at[s], v_sems.at[s]) for s in range(4)]
    for fetch in [fetch_w] + fetch_v + [fetch_table]:
        fetch.start()
    order = row_order(32, 16)
    fetch_w.wait()
    w = w_ref[...]
    below = jnp.concatenate([jnp.zeros((288, 64), BF), w[:288]], 0)
    wt_ref[...] = turned(jnp.concatenate([w[288:], below], 1)).astype(BF)
    wt0_ref[...] = turned(w[:288]).astype(BF)
    for s in range(4):
        fetch_v[s].wait()
        rows = dot(order, v_ref[s].reshape(512, 512)).astype(BF)
        rows_ref[s] = rows
        rim_ref[s] = rows[480:]
    fetch_table.wait()


def first_body(rows_ref, table_ref, wt_ref, im_hbm, pre_ref, z_ref, im_ref, im_sems):
    def one(s, carry):
        z_ref[...] = dot(rows_ref[s], table_ref[...])
        for half in range(2):
            for o1 in range(8):
                at = (half * 8 + o1) * 32
                for t, tap in enumerate(spread(z_ref[at : at + 32], 8, 128)):
                    k = (9 * half + t) * 32
                    im_ref[s, k : k + 32, o1 * LANES : (o1 + 1) * LANES] = tap.astype(BF)
        pltpu.make_async_copy(im_ref.at[s], im_hbm.at[s], im_sems.at[s]).start()
        got = dot(wt_ref[...], im_ref[s])
        pre_ref[s, :, :LANES] = got[:64, :LANES]
        pre_ref[s, :, LANES:] = got[:64, LANES:] + got[64:, :-LANES]
        return carry

    lax.fori_loop(0, 4, one, 0)
    for s in range(4):
        pltpu.make_async_copy(im_ref.at[s], im_hbm.at[s], im_sems.at[s]).wait()


def rim_body(
    me_ref, up_hbm, pre_ref, rim_ref, table_ref, wt0_ref, hid_ref, send_ref, send2, send3, own_ref, slope_ref, rimz_ref, up_ref, sem
):
    fetch = pltpu.make_async_copy(up_hbm, up_ref, sem)
    fetch.start()
    taps = spread(dot(rim_ref[...].reshape(128, 512), table_ref[...]), 8, 128)
    for s in range(4):
        im = jnp.concatenate([tap[32 * s : 32 * s + 32] for tap in taps], 0).astype(BF)
        rimz_ref[s] = im
        extra = dot(wt0_ref[...], im)
        for r in range(8):
            lanes = slice(r * LANES, (r + 1) * LANES)
            pre = pre_ref[s, :, lanes]
            if r == 0:
                pre = pre + extra
            act, slope = act_and_slope(pre)
            hidden = act.astype(BF)
            hid_ref[s, :, lanes] = hidden
            slope_ref[s, :, lanes] = slope
            if r == 7:
                send_ref[64 * s : 64 * s + 64] = hidden
    fetch.wait()
    me = me_ref[0]
    send_ref[256:] = up_ref[(me + 1) & 3]
    send2[...] = up_ref[(me + 2) & 3]
    send3[...] = up_ref[(me + 3) & 3]
    own_ref[...] = up_ref[me]


def second_body(hid_ref, table_ref, w_ref, im_ref, pre_ref):
    for s in range(4):
        row = lambda r: (
            hid_ref[s, :, r * LANES : (r + 1) * LANES] if r >= 0 else jnp.zeros((64, LANES), BF)
        )
        left = jnp.concatenate(
            [jnp.concatenate([row(2 * o1 + a - 1) for o1 in range(4)], 1) for a in range(3)], 0
        )
        for t, tap in enumerate(spread(dot(left, table_ref[...]), 4, 32)):
            for a in range(3):
                k = (9 * a + t) * 64
                im_ref[k : k + 64, s * LANES : (s + 1) * LANES] = tap[
                    64 * a : 64 * a + 64
                ].astype(BF)
    pre_ref[...] = dot(turned(w_ref[...]).astype(BF), im_ref[...])


def halo_body(me_ref, got_ref, pre_ref, own_ref, got2, got3, table_ref, w_ref, *refs):
    send_ref, send2, send3, kept_ref, delta_ref, imh_ref, up_ref, feat_ref = refs
    me = me_ref[0]
    up_ref[me] = own_ref[...]
    up_ref[(me + 1) & 3] = got3[...]
    up_ref[(me + 2) & 3] = got2[...]
    up_ref[(me + 3) & 3] = got_ref[256:]
    z = dot(got_ref[:256], table_ref[:LANES, :])
    for t, tap in enumerate(spread(jnp.where(me > 0, z, 0.0), 4, 32)):
        for s in range(4):
            imh_ref[t * 64 : t * 64 + 64, s * LANES : (s + 1) * LANES] = tap[
                64 * s : 64 * s + 64
            ].astype(BF)
    pre = pre_ref[...] + dot(turned(w_ref[:576]).astype(BF), imh_ref[...])
    lane = lax.broadcasted_iota(jnp.int32, (128, LANES), 1)
    edge = jnp.zeros((128, LANES), F32)
    for s in range(4):
        act, slope = act_and_slope(pre[:, s * LANES : (s + 1) * LANES])
        feat_ref[s] = turned(act.astype(BF)).astype(BF)
        delta = (turned(up_ref[s]) * slope).astype(BF)
        delta_ref[s] = delta
        moved = delta.astype(F32)
        if s:
            moved = pltpu.roll(moved, 32 * s, 1)
        edge = jnp.where(lane // 32 == s, moved, edge)
    send_ref[:128] = edge.astype(BF)
    send_ref[128:] = feat_ref[(me + 3) & 3]
    send2[...] = feat_ref[(me + 2) & 3]
    send3[...] = feat_ref[(me + 1) & 3]
    kept_ref[...] = feat_ref[me]


def split_halves(me_ref, all_ref, keep_ref, send_ref):
    half = keep_ref.shape[0]
    core = me_ref[0] & 1
    keep_ref[...] = all_ref[pl.ds(pl.multiple_of(core * half, 8), half), :]
    send_ref[...] = all_ref[pl.ds(pl.multiple_of((1 - core) * half, 8), half), :].astype(BF)


def second_grad_body(me_ref, im_ref, imh_ref, delta_ref, keep_ref, send_ref, all_ref):
    scale = 1.0 / 256
    delta = jnp.concatenate([delta_ref[s] for s in range(4)], 1)
    all_ref[:576] = dot_nt(im_ref[:576] + imh_ref[...], delta) * scale
    all_ref[576:] = dot_nt(im_ref[576:], delta) * scale
    split_halves(me_ref, all_ref, keep_ref, send_ref)


def join_body(wide_ref, got_wide, packed_ref, got_packed, out_ref):
    out_ref[:864] = (wide_ref[...] + got_wide[...].astype(F32)).astype(BF)
    packed = packed_ref[...] + got_packed[...].astype(F32)
    out_ref[864:] = jnp.concatenate([packed, jnp.zeros((72, LANES), F32)], 0).astype(BF)


def back_body(
    me_ref, im_hbm, delta_ref, got_ref, k_ref, table_ref, slope_ref, rimz_ref, keep_ref, send_ref, kodd_ref, ahead_ref, acc_ref, all_ref, im_ref, sems
):
    for s in range(4):
        pltpu.make_async_copy(im_hbm.at[s], im_ref.at[s], sems.at[s]).start()
    lane = lax.broadcasted_iota(jnp.int32, (128, LANES), 1)
    acc_ref[...] = jnp.zeros_like(acc_ref)
    kodd_ref[:, :128] = k_ref[:576]
    kodd_ref[:, 128:] = k_ref[1152:]
    rim = jnp.where(me_ref[0] < 3, got_ref[:128].astype(F32), 0.0)
    for s in range(4):
        own = delta_ref[s]
        moved = pltpu.roll(own.astype(F32), 96, 1)
        ends = pltpu.roll(rim, 96 - 32 * s, 1) if s != 3 else rim
        ahead_ref[s, :128] = jnp.where(lane < 96, moved, ends).astype(BF)
        ahead_ref[s, 128:] = own

    def one(s, carry):
        even = dot(k_ref[576:1152], delta_ref[s])
        odd = dot(kodd_ref[...], ahead_ref[s])
        parts = []
        for grad in (even, odd):
            flat = collect([grad[64 * t : 64 * t + 64] for t in range(9)], 4, 32)
            high = flat.astype(BF)
            parts += [high, (flat - high.astype(F32)).astype(BF)]
        got = dot_nt(jnp.concatenate(parts, 0), table_ref[...])
        rows = []
        for r in range(8):
            base = 128 * (r % 2)
            lanes = slice((r // 2) * LANES, (r // 2 + 1) * LANES)
            back = (got[base : base + 64, lanes] + got[base + 64 : base + 128, lanes]).astype(BF)
            slope = slope_ref[s, :, r * LANES : (r + 1) * LANES]
            rows.append((back.astype(F32) * slope).astype(BF))
        zero = jnp.zeros((64, LANES), BF)
        both = jnp.concatenate(
            [jnp.concatenate(rows, 1), jnp.concatenate(rows[1:] + [zero], 1)], 0
        )
        pltpu.make_async_copy(im_hbm.at[s], im_ref.at[s], sems.at[s]).wait()
        acc_ref[...] += dot_nt(im_ref[s], both)
        acc_ref[288:] += dot_nt(rimz_ref[s], jnp.concatenate([zero, rows[0]], 0))
        return carry

    lax.fori_loop(0, 4, one, 0)
    acc = acc_ref[...] * (1.0 / 256)
    all_ref[:288] = acc[288:]
    all_ref[288:] = jnp.concatenate([acc[:144, :64], acc[144:288, :64]], 1)
    split_halves(me_ref, all_ref, keep_ref, send_ref)


def finish_body(me_ref, rows_ref, other_ref, kept_ref, got_ref, got2, got3, first_ref, second_ref, feat_ref):
    me = me_ref[0]
    feat_ref[me] = kept_ref[...]
    feat_ref[(me + 1) & 3] = got_ref[128:]
    feat_ref[(me + 2) & 3] = got2[...]
    feat_ref[(me + 3) & 3] = got3[...]
    mine, other = rows_ref[...].astype(F32), other_ref[...].astype(F32)
    front = jnp.where((me & 1) == 0, mine, other)
    back = jnp.where((me & 1) == 0, other, mine)
    second_ref[:864] = front[:864]
    second_ref[864:] = back[:864]
    low, high = front[864:1080], back[864:1080]
    odd = jnp.concatenate([low, high[:72]], 0)
    even = high[72:216]
    first_ref[:288] = odd[:, 64:]
    first_ref[288:432] = even[:, :64]
    first_ref[432:576] = even[:, 64:]
    first_ref[576:] = odd[:, :64]


def call(body, outs, scratch=(), mib=24, final=False, far=(), far_outs=()):
    here = pl.BlockSpec(memory_space=pltpu.VMEM)
    there = pl.BlockSpec(memory_space=pl.ANY if INTERPRET else pltpu.HBM)
    scalar = pl.BlockSpec(memory_space=pltpu.SMEM)

    def shape_of(at, out):
        if INTERPRET or final:
            return jax.ShapeDtypeStruct(*out)
        return pltpu.HBM(*out) if at in far_outs else pltpu.VMEM(*out)

    def run(*args):
        if not INTERPRET:
            args = [
                pltpu.with_memory_space_constraint(arg, pltpu.HBM) if at in far else arg
                for at, arg in enumerate(args)
            ]
        return pl.pallas_call(
            body,
            in_specs=[
                scalar if arg.shape == (1,) else there if at in far else here
                for at, arg in enumerate(args)
            ],
            out_specs=[there if at in far_outs else here for at in range(len(outs))],
            out_shape=[shape_of(at, out) for at, out in enumerate(outs)],
            scratch_shapes=list(scratch),
            compiler_params=pltpu.CompilerParams(vmem_limit_bytes=mib * 1024 * 1024),
            interpret=INTERPRET,
        )(*args)

    return run


def exchange(chunks, axis):
    return lax.all_to_all(chunks, axis, split_axis=0, concat_axis=0, tiled=True)


def reduce_stage(rows, axis):
    got = exchange(rows.reshape(lax.axis_size(axis), -1, LANES), axis)
    return jnp.sum(got.astype(F32), 0).astype(BF)


def gather_stage(rows, axis):
    copies = jnp.broadcast_to(rows[None], (lax.axis_size(axis),) + rows.shape)
    return exchange(copies, axis).reshape(-1, LANES)


def sum_everywhere(rows):
    rows = reduce_stage(rows, XY_GROUP)
    got = exchange(jnp.broadcast_to(rows[None], (lax.axis_size("z"),) + rows.shape), "z")
    rows = jnp.sum(got.astype(F32), 0).astype(BF)
    return gather_stage(rows, XY_GROUP)


def across(value):
    return lax.ppermute(value, "c", [(0, 1), (1, 0)])


def rotated(value, steps):
    return lax.ppermute(value, SPACE, [(i, (i + steps) % 4) for i in range(4)])


def per_device(volumes, first_kernel, second_kernel, upstream):
    me = lax.axis_index(SPACE).reshape(1)
    tile = ((128, 128), BF)
    table = phase_table(YD, ZD, 1)
    table2 = phase_table(YD // 2, ZD // 2, 4)
    k2 = second_kernel.reshape(1728, 128)
    up = upstream.reshape(128, 4, 128).transpose(1, 2, 0)
    rows, rim, wt, wt0, near_table = call(
        load_body,
        [
            ((4, 512, 512), BF),
            ((4, 32, 512), BF),
            ((128, 576), BF),
            ((64, 288), BF),
            ((512, 512), BF),
        ],
        scratch=[
            pltpu.VMEM((4, 32, 16, 512), BF),
            pltpu.VMEM((864, 64), BF),
            pltpu.SemaphoreType.DMA((2,)),
            pltpu.SemaphoreType.DMA((4,)),
        ],
        far=(0, 1, 2),
    )(volumes, first_kernel.reshape(864, 64), table)
    rim = shifted(rim, SPACE, 1)
    im1, pre1 = call(
        first_body,
        [((4, 576, 1024), BF), ((4, 64, 1024), F32)],
        scratch=[
            pltpu.VMEM((512, 512), F32),
            pltpu.VMEM((4, 576, 1024), BF),
            pltpu.SemaphoreType.DMA((4,)),
        ],
        far_outs=(0,),
    )(rows, near_table, wt)
    hidden, sent, sent2, sent3, own, slope1, rimz = call(
        rim_body,
        [
            ((4, 64, 1024), BF),
            ((384, 128), BF),
            tile,
            tile,
            tile,
            ((4, 64, 1024), F32),
            ((4, 288, 128), BF),
        ],
        scratch=[pltpu.VMEM((4, 128, 128), BF), pltpu.SemaphoreType.DMA(())],
        far=(1,),
    )(me, up, pre1, rim, table, wt0)
    got = rotated(sent, 1)
    got2 = rotated(sent2, 2)
    got3 = rotated(sent3, 3)
    im2, pre2 = call(second_body, [((1728, 512), BF), ((128, 512), F32)])(hidden, table2, k2)
    sent, sent2, sent3, kept, delta2, im2h = call(
        halo_body,
        [((256, 128), BF), tile, tile, tile, ((4, 128, 128), BF), ((576, 512), BF)],
        scratch=[pltpu.VMEM((4, 128, 128), BF), pltpu.VMEM((4, 128, 128), BF)],
    )(me, got, pre2, own, got2, got3, table2, k2)
    got = rotated(sent, 3)
    got2 = rotated(sent2, 2)
    got3 = rotated(sent3, 1)
    wide, wide_out = call(
        second_grad_body,
        [((864, 128), F32), ((864, 128), BF)],
        scratch=[pltpu.VMEM((1728, 128), F32)],
    )(me, im2, im2h, delta2)
    packed, packed_out = call(
        back_body,
        [((216, 128), F32), ((216, 128), BF)],
        scratch=[
            pltpu.VMEM((576, 256), BF),
            pltpu.VMEM((4, 256, 128), BF),
            pltpu.VMEM((576, 128), F32),
            pltpu.VMEM((432, 128), F32),
            pltpu.VMEM((4, 576, 1024), BF),
            pltpu.SemaphoreType.DMA((4,)),
        ],
        far=(1,),
    )(me, im1, delta2, got, k2, table2, slope1, rimz)
    packed, packed_out, got2, got3 = lax.optimization_barrier((packed, packed_out, got2, got3))
    (rows,) = call(join_body, [((1152, 128), BF)])(
        wide, across(wide_out), packed, across(packed_out)
    )
    rows = sum_everywhere(rows)
    first_grad, second_grad, features = call(
        finish_body,
        [((864, 64), F32), ((1728, 128), F32), ((4, 128, 128), BF)],
        final=True,
    )(me, rows, across(rows), kept, got, got2, got3)
    features = features.transpose(2, 0, 1).reshape(1, 128, 16, 32)
    return (features, first_grad.reshape(27, 32, 64), second_grad.reshape(27, 64, 128))


def solution(mesh):
    fine = Mesh(mesh.devices.reshape(4, 8, 2, 2, 2), ("y", "z", "xl", "xh", "c"))
    in_specs = (P(DP, None, SPACE, None), P(), P(), P(DP + SPACE, None, None, None))
    out_specs = (P(DP + SPACE, None, None, None), P(), P())
    return jax.shard_map(
        per_device, mesh=fine, in_specs=in_specs, out_specs=out_specs, check_vma=False
    )
```

```python
import jax
import jax.numpy as jnp
import numpy as np
from jax import lax
from jax.experimental import pallas as pl
from jax.experimental.pallas import tpu as pltpu
from jax.sharding import Mesh
from jax.sharding import PartitionSpec as P

YD = 32
ZD = 16
LANES = 128
DP = ("y", "z", "xl")
SPACE = ("xh", "c")
XY_GROUP = ("y", "xl", "xh")
BF = jnp.bfloat16
F32 = jnp.float32
INTERPRET = False


def shifted(value, axis, steps):
    count = lax.axis_size(axis)
    initial, last = (max(0, -steps), min(count, count - steps))
    return lax.ppermute(value, axis, [(source, source + steps) for source in range(initial, last)])


def phase_table(size_y, size_z, copies):
    shape = (copies, size_y // 2, 2, size_z // 2, 2)
    at = np.arange(np.prod(shape)).reshape(shape).transpose(2, 4, 0, 1, 3).reshape(-1)
    return jnp.asarray(np.eye(at.size, dtype=np.float32)[:, at], BF)


def tap_masks(shape, row, cells):
    lane = lax.broadcasted_iota(jnp.int32, shape, 1) % cells
    return lane >= row, lane % row != 0


def tap_parts(row):
    for second in range(3):
        for third in range(3):
            back_y, back_z = second == 0, third == 0
            yield 2 * (second != 1) + (third != 1), row * back_y + back_z, back_y, back_z


def spread(phases, row, cells):
    in_y, in_z = tap_masks((phases.shape[0], LANES), row, cells)
    taps = []
    for phase, steps, back_y, back_z in tap_parts(row):
        tap = phases[:, phase * LANES : (phase + 1) * LANES]
        if steps:
            mask = in_y & in_z if back_y and back_z else in_y if back_y else in_z
            tap = jnp.where(mask, pltpu.roll(tap, steps, 1), 0.0)
        taps.append(tap)
    return taps


def collect(taps, row, cells):
    in_y, in_z = tap_masks(taps[0].shape, row, cells)
    phases = [None] * 4
    for tap, (phase, steps, back_y, back_z) in zip(taps, tap_parts(row)):
        if steps:
            mask = in_y & in_z if back_y and back_z else in_y if back_y else in_z
            tap = pltpu.roll(jnp.where(mask, tap, 0.0), LANES - steps, 1)
        phases[phase] = tap if phases[phase] is None else phases[phase] + tap
    return jnp.concatenate(phases, 1)


def row_order(chans, rows):
    shape = (rows * chans, chans * rows)
    at = lax.broadcasted_iota(jnp.int32, shape, 0)
    source = lax.broadcasted_iota(jnp.int32, shape, 1)
    block = at // chans
    row = (block % (rows // 2)) * 2 + block // (rows // 2)
    return (source == (at % chans) * rows + row).astype(F32).astype(BF)


def turned(value):
    size = value.shape[1]
    row = lax.broadcasted_iota(jnp.int32, (size, size), 0)
    col = lax.broadcasted_iota(jnp.int32, (size, size), 1)
    return dot_nt((row == col).astype(F32).astype(BF), value)


def dot(a, b):
    return jnp.dot(a, b, preferred_element_type=F32)


def dot_nt(a, b):
    return lax.dot_general(a, b, (((1,), (1,)), ((), ())), preferred_element_type=F32)


def act_and_slope(v):
    e = jnp.exp(-jnp.abs(v))
    act = 0.3 * v + 0.7 * (jnp.maximum(v, 0.0) + jnp.log(1.0 + e))
    slope = 0.3 + 0.7 * jnp.where(v >= 0, 1.0, e) / (1.0 + e)
    return act, slope


def load_body(
    v_hbm, w_hbm, table_hbm, rows_ref, rim_ref, wt_ref, wt0_ref, table_ref, v_ref, w_ref, sems, v_sems
):
    fetch_w = pltpu.make_async_copy(w_hbm, w_ref, sems.at[0])
    fetch_table = pltpu.make_async_copy(table_hbm, table_ref, sems.at[1])
    fetch_v = [pltpu.make_async_copy(v_hbm.at[s], v_ref.at[s], v_sems.at[s]) for s in range(4)]
    for fetch in [fetch_w] + fetch_v + [fetch_table]:
        fetch.start()
    order = row_order(32, 16)
    fetch_w.wait()
    w = w_ref[...]
    below = jnp.concatenate([jnp.zeros((288, 64), BF), w[:288]], 0)
    wt_ref[...] = turned(jnp.concatenate([w[288:], below], 1)).astype(BF)
    wt0_ref[...] = turned(w[:288]).astype(BF)
    for s in range(4):
        fetch_v[s].wait()
        rows = dot(order, v_ref[s].reshape(512, 512)).astype(BF)
        rows_ref[s] = rows
        rim_ref[s] = rows[480:]
    fetch_table.wait()


def first_body(rows_ref, table_ref, wt_ref, im_hbm, pre_ref, z_ref, im_ref, im_sems):
    def one(s, carry):
        z_ref[...] = dot(rows_ref[s], table_ref[...])
        for half in range(2):
            for o1 in range(8):
                at = (half * 8 + o1) * 32
                for t, tap in enumerate(spread(z_ref[at : at + 32], 8, 128)):
                    k = (9 * half + t) * 32
                    im_ref[s, k : k + 32, o1 * LANES : (o1 + 1) * LANES] = tap.astype(BF)
        pltpu.make_async_copy(im_ref.at[s], im_hbm.at[s], im_sems.at[s]).start()
        got = dot(wt_ref[...], im_ref[s])
        pre_ref[s, :, :LANES] = got[:64, :LANES]
        pre_ref[s, :, LANES:] = got[:64, LANES:] + got[64:, :-LANES]
        return carry

    lax.fori_loop(0, 4, one, 0)
    for s in range(4):
        pltpu.make_async_copy(im_ref.at[s], im_hbm.at[s], im_sems.at[s]).wait()


def rim_body(
    me_ref, up_hbm, pre_ref, rim_ref, table_ref, wt0_ref, hid_ref, send_ref, send2, send3, own_ref, slope_ref, rimz_ref, up_ref, sem
):
    fetch = pltpu.make_async_copy(up_hbm, up_ref, sem)
    fetch.start()
    taps = spread(dot(rim_ref[...].reshape(128, 512), table_ref[...]), 8, 128)
    for s in range(4):
        im = jnp.concatenate([tap[32 * s : 32 * s + 32] for tap in taps], 0).astype(BF)
        rimz_ref[s] = im
        extra = dot(wt0_ref[...], im)
        for r in range(8):
            lanes = slice(r * LANES, (r + 1) * LANES)
            pre = pre_ref[s, :, lanes]
            if r == 0:
                pre = pre + extra
            act, slope = act_and_slope(pre)
            hidden = act.astype(BF)
            hid_ref[s, :, lanes] = hidden
            slope_ref[s, :, lanes] = slope
            if r == 7:
                send_ref[64 * s : 64 * s + 64] = hidden
    fetch.wait()
    me = me_ref[0]
    send_ref[256:] = up_ref[(me + 1) & 3]
    send2[...] = up_ref[(me + 2) & 3]
    send3[...] = up_ref[(me + 3) & 3]
    own_ref[...] = up_ref[me]


def second_body(hid_ref, table_ref, w_ref, im_ref, pre_ref):
    for s in range(4):
        row = lambda r: (
            hid_ref[s, :, r * LANES : (r + 1) * LANES] if r >= 0 else jnp.zeros((64, LANES), BF)
        )
        left = jnp.concatenate(
            [jnp.concatenate([row(2 * o1 + a - 1) for o1 in range(4)], 1) for a in range(3)], 0
        )
        for t, tap in enumerate(spread(dot(left, table_ref[...]), 4, 32)):
            for a in range(3):
                k = (9 * a + t) * 64
                im_ref[k : k + 64, s * LANES : (s + 1) * LANES] = tap[
                    64 * a : 64 * a + 64
                ].astype(BF)
    pre_ref[...] = dot(turned(w_ref[...]).astype(BF), im_ref[...])


def halo_body(me_ref, got_ref, pre_ref, own_ref, got2, got3, table_ref, w_ref, *refs):
    send_ref, send2, send3, kept_ref, delta_ref, imh_ref, up_ref, feat_ref = refs
    me = me_ref[0]
    up_ref[me] = own_ref[...]
    up_ref[(me + 1) & 3] = got3[...]
    up_ref[(me + 2) & 3] = got2[...]
    up_ref[(me + 3) & 3] = got_ref[256:]
    z = dot(got_ref[:256], table_ref[:LANES, :])
    for t, tap in enumerate(spread(jnp.where(me > 0, z, 0.0), 4, 32)):
        for s in range(4):
            imh_ref[t * 64 : t * 64 + 64, s * LANES : (s + 1) * LANES] = tap[
                64 * s : 64 * s + 64
            ].astype(BF)
    pre = pre_ref[...] + dot(turned(w_ref[:576]).astype(BF), imh_ref[...])
    lane = lax.broadcasted_iota(jnp.int32, (128, LANES), 1)
    edge = jnp.zeros((128, LANES), F32)
    for s in range(4):
        act, slope = act_and_slope(pre[:, s * LANES : (s + 1) * LANES])
        feat_ref[s] = turned(act.astype(BF)).astype(BF)
        delta = (turned(up_ref[s]) * slope).astype(BF)
        delta_ref[s] = delta
        moved = delta.astype(F32)
        if s:
            moved = pltpu.roll(moved, 32 * s, 1)
        edge = jnp.where(lane // 32 == s, moved, edge)
    send_ref[:128] = edge.astype(BF)
    send_ref[128:] = feat_ref[(me + 3) & 3]
    send2[...] = feat_ref[(me + 2) & 3]
    send3[...] = feat_ref[(me + 1) & 3]
    kept_ref[...] = feat_ref[me]


def split_halves(me_ref, all_ref, keep_ref, send_ref):
    half = keep_ref.shape[0]
    core = me_ref[0] & 1
    keep_ref[...] = all_ref[pl.ds(pl.multiple_of(core * half, 8), half), :]
    send_ref[...] = all_ref[pl.ds(pl.multiple_of((1 - core) * half, 8), half), :].astype(BF)


def second_grad_body(me_ref, im_ref, imh_ref, delta_ref, keep_ref, send_ref, all_ref):
    scale = 1.0 / 256
    delta = jnp.concatenate([delta_ref[s] for s in range(4)], 1)
    all_ref[:576] = dot_nt(im_ref[:576] + imh_ref[...], delta) * scale
    all_ref[576:] = dot_nt(im_ref[576:], delta) * scale
    split_halves(me_ref, all_ref, keep_ref, send_ref)


def join_body(wide_ref, got_wide, packed_ref, got_packed, out_ref):
    out_ref[:864] = (wide_ref[...] + got_wide[...].astype(F32)).astype(BF)
    packed = packed_ref[...] + got_packed[...].astype(F32)
    out_ref[864:] = jnp.concatenate([packed, jnp.zeros((72, LANES), F32)], 0).astype(BF)


def back_body(
    me_ref, im_hbm, delta_ref, got_ref, k_ref, table_ref, slope_ref, rimz_ref, keep_ref, send_ref, kodd_ref, ahead_ref, acc_ref, all_ref, im_ref, sems
):
    for s in range(4):
        pltpu.make_async_copy(im_hbm.at[s], im_ref.at[s], sems.at[s]).start()
    lane = lax.broadcasted_iota(jnp.int32, (128, LANES), 1)
    acc_ref[...] = jnp.zeros_like(acc_ref)
    kodd_ref[:, :128] = k_ref[:576]
    kodd_ref[:, 128:] = k_ref[1152:]
    rim = jnp.where(me_ref[0] < 3, got_ref[:128].astype(F32), 0.0)
    for s in range(4):
        own = delta_ref[s]
        moved = pltpu.roll(own.astype(F32), 96, 1)
        ends = pltpu.roll(rim, 96 - 32 * s, 1) if s != 3 else rim
        ahead_ref[s, :128] = jnp.where(lane < 96, moved, ends).astype(BF)
        ahead_ref[s, 128:] = own

    def one(s, carry):
        even = dot(k_ref[576:1152], delta_ref[s])
        odd = dot(kodd_ref[...], ahead_ref[s])
        parts = []
        for grad in (even, odd):
            flat = collect([grad[64 * t : 64 * t + 64] for t in range(9)], 4, 32)
            high = flat.astype(BF)
            parts += [high, (flat - high.astype(F32)).astype(BF)]
        got = dot_nt(jnp.concatenate(parts, 0), table_ref[...])
        rows = []
        for r in range(8):
            base = 128 * (r % 2)
            lanes = slice((r // 2) * LANES, (r // 2 + 1) * LANES)
            back = (got[base : base + 64, lanes] + got[base + 64 : base + 128, lanes]).astype(BF)
            slope = slope_ref[s, :, r * LANES : (r + 1) * LANES]
            rows.append((back.astype(F32) * slope).astype(BF))
        zero = jnp.zeros((64, LANES), BF)
        both = jnp.concatenate(
            [jnp.concatenate(rows, 1), jnp.concatenate(rows[1:] + [zero], 1)], 0
        )
        pltpu.make_async_copy(im_hbm.at[s], im_ref.at[s], sems.at[s]).wait()
        acc_ref[...] += dot_nt(im_ref[s], both)
        acc_ref[288:] += dot_nt(rimz_ref[s], jnp.concatenate([zero, rows[0]], 0))
        return carry

    lax.fori_loop(0, 4, one, 0)
    acc = acc_ref[...] * (1.0 / 256)
    all_ref[:288] = acc[288:]
    all_ref[288:] = jnp.concatenate([acc[:144, :64], acc[144:288, :64]], 1)
    split_halves(me_ref, all_ref, keep_ref, send_ref)


def finish_body(me_ref, rows_ref, other_ref, kept_ref, got_ref, got2, got3, first_ref, second_ref, feat_ref):
    me = me_ref[0]
    feat_ref[me] = kept_ref[...]
    feat_ref[(me + 1) & 3] = got_ref[128:]
    feat_ref[(me + 2) & 3] = got2[...]
    feat_ref[(me + 3) & 3] = got3[...]
    mine, other = rows_ref[...].astype(F32), other_ref[...].astype(F32)
    front = jnp.where((me & 1) == 0, mine, other)
    back = jnp.where((me & 1) == 0, other, mine)
    second_ref[:864] = front[:864]
    second_ref[864:] = back[:864]
    low, high = front[864:1080], back[864:1080]
    odd = jnp.concatenate([low, high[:72]], 0)
    even = high[72:216]
    first_ref[:288] = odd[:, 64:]
    first_ref[288:432] = even[:, :64]
    first_ref[432:576] = even[:, 64:]
    first_ref[576:] = odd[:, :64]


def call(body, outs, scratch=(), mib=24, final=False, far=(), far_outs=()):
    here = pl.BlockSpec(memory_space=pltpu.VMEM)
    there = pl.BlockSpec(memory_space=pl.ANY if INTERPRET else pltpu.HBM)
    scalar = pl.BlockSpec(memory_space=pltpu.SMEM)

    def shape_of(at, out):
        if INTERPRET or final:
            return jax.ShapeDtypeStruct(*out)
        return pltpu.HBM(*out) if at in far_outs else pltpu.VMEM(*out)

    def run(*args):
        if not INTERPRET:
            args = [
                pltpu.with_memory_space_constraint(arg, pltpu.HBM) if at in far else arg
                for at, arg in enumerate(args)
            ]
        return pl.pallas_call(
            body,
            in_specs=[
                scalar if arg.shape == (1,) else there if at in far else here
                for at, arg in enumerate(args)
            ],
            out_specs=[there if at in far_outs else here for at in range(len(outs))],
            out_shape=[shape_of(at, out) for at, out in enumerate(outs)],
            scratch_shapes=list(scratch),
            compiler_params=pltpu.CompilerParams(vmem_limit_bytes=mib * 1024 * 1024),
            interpret=INTERPRET,
        )(*args)

    return run


def exchange(chunks, axis):
    return lax.all_to_all(chunks, axis, split_axis=0, concat_axis=0, tiled=True)


def reduce_stage(rows, axis):
    got = exchange(rows.reshape(lax.axis_size(axis), -1, LANES), axis)
    return jnp.sum(got.astype(F32), 0).astype(BF)


def gather_stage(rows, axis):
    copies = jnp.broadcast_to(rows[None], (lax.axis_size(axis),) + rows.shape)
    return exchange(copies, axis).reshape(-1, LANES)


def sum_everywhere(rows):
    rows = reduce_stage(rows, XY_GROUP)
    rows = rows.astype(F32)
    count = lax.axis_size("z")
    steps = [[place ^ step for place in range(count)] for step in (1, 2) if 2 * step < count]
    for peers in steps + [[count - 1 - place for place in range(count)]] * (count > 1):
        sent = rows if peers in steps else rows.astype(BF)
        got = lax.ppermute(sent, "z", list(enumerate(peers)))
        rows = sent.astype(F32) + got.astype(F32)
    rows = rows.astype(BF)
    return gather_stage(rows, XY_GROUP)


def across(value):
    return lax.ppermute(value, "c", [(0, 1), (1, 0)])


def rotated(value, steps):
    return lax.ppermute(value, SPACE, [(i, (i + steps) % 4) for i in range(4)])


def per_device(volumes, first_kernel, second_kernel, upstream):
    me = lax.axis_index(SPACE).reshape(1)
    tile = ((128, 128), BF)
    table = phase_table(YD, ZD, 1)
    table2 = phase_table(YD // 2, ZD // 2, 4)
    k2 = second_kernel.reshape(1728, 128)
    up = upstream.reshape(128, 4, 128).transpose(1, 2, 0)
    rows, rim, wt, wt0, near_table = call(
        load_body,
        [
            ((4, 512, 512), BF),
            ((4, 32, 512), BF),
            ((128, 576), BF),
            ((64, 288), BF),
            ((512, 512), BF),
        ],
        scratch=[
            pltpu.VMEM((4, 32, 16, 512), BF),
            pltpu.VMEM((864, 64), BF),
            pltpu.SemaphoreType.DMA((2,)),
            pltpu.SemaphoreType.DMA((4,)),
        ],
        far=(0, 1, 2),
    )(volumes, first_kernel.reshape(864, 64), table)
    rim = shifted(rim, SPACE, 1)
    im1, pre1 = call(
        first_body,
        [((4, 576, 1024), BF), ((4, 64, 1024), F32)],
        scratch=[
            pltpu.VMEM((512, 512), F32),
            pltpu.VMEM((4, 576, 1024), BF),
            pltpu.SemaphoreType.DMA((4,)),
        ],
        far_outs=(0,),
    )(rows, near_table, wt)
    hidden, sent, sent2, sent3, own, slope1, rimz = call(
        rim_body,
        [
            ((4, 64, 1024), BF),
            ((384, 128), BF),
            tile,
            tile,
            tile,
            ((4, 64, 1024), F32),
            ((4, 288, 128), BF),
        ],
        scratch=[pltpu.VMEM((4, 128, 128), BF), pltpu.SemaphoreType.DMA(())],
        far=(1,),
    )(me, up, pre1, rim, table, wt0)
    got = rotated(sent, 1)
    got2 = rotated(sent2, 2)
    got3 = rotated(sent3, 3)
    im2, pre2 = call(second_body, [((1728, 512), BF), ((128, 512), F32)])(hidden, table2, k2)
    sent, sent2, sent3, kept, delta2, im2h = call(
        halo_body,
        [((256, 128), BF), tile, tile, tile, ((4, 128, 128), BF), ((576, 512), BF)],
        scratch=[pltpu.VMEM((4, 128, 128), BF), pltpu.VMEM((4, 128, 128), BF)],
    )(me, got, pre2, own, got2, got3, table2, k2)
    got = rotated(sent, 3)
    got2 = rotated(sent2, 2)
    got3 = rotated(sent3, 1)
    wide, wide_out = call(
        second_grad_body,
        [((864, 128), F32), ((864, 128), BF)],
        scratch=[pltpu.VMEM((1728, 128), F32)],
    )(me, im2, im2h, delta2)
    packed, packed_out = call(
        back_body,
        [((216, 128), F32), ((216, 128), BF)],
        scratch=[
            pltpu.VMEM((576, 256), BF),
            pltpu.VMEM((4, 256, 128), BF),
            pltpu.VMEM((576, 128), F32),
            pltpu.VMEM((432, 128), F32),
            pltpu.VMEM((4, 576, 1024), BF),
            pltpu.SemaphoreType.DMA((4,)),
        ],
        far=(1,),
    )(me, im1, delta2, got, k2, table2, slope1, rimz)
    packed, packed_out, got2, got3 = lax.optimization_barrier((packed, packed_out, got2, got3))
    (rows,) = call(join_body, [((1152, 128), BF)])(
        wide, across(wide_out), packed, across(packed_out)
    )
    rows = sum_everywhere(rows)
    first_grad, second_grad, features = call(
        finish_body,
        [((864, 64), F32), ((1728, 128), F32), ((4, 128, 128), BF)],
        final=True,
    )(me, rows, across(rows), kept, got, got2, got3)
    features = features.transpose(2, 0, 1).reshape(1, 128, 16, 32)
    return (features, first_grad.reshape(27, 32, 64), second_grad.reshape(27, 64, 128))


def solution(mesh):
    fine = Mesh(mesh.devices.reshape(4, 8, 2, 2, 2), ("y", "z", "xl", "xh", "c"))
    in_specs = (P(DP, None, SPACE, None), P(), P(), P(DP + SPACE, None, None, None))
    out_specs = (P(DP + SPACE, None, None, None), P(), P())
    return jax.shard_map(
        per_device, mesh=fine, in_specs=in_specs, out_specs=out_specs, check_vma=False
    )
```
